256 devices in a mesh: seq: 64 (over y, z, core), head: 4 (over x).
Axes of the slice: x: 4, y: 4, z: 8, core: 2. Of those that a mesh axis runs over, the one named last changes fastest.
Arguments:
- tokens: bfloat16 [131072, 2048], P(('seq', 'head')), may hold values from -60 to 60
- query_index: int32 [8192], replicated, may hold values from 0 to 131071, as said below
- key_index: int32 [8192], replicated, may hold values from 0 to 131071, as said below
- light_query: bfloat16 [2048, 256], replicated, may hold values from -0.1875 to 0.1875
- light_key: bfloat16 [2048, 256], replicated, may hold values from -0.1875 to 0.1875
- light_value: bfloat16 [2048, 256], replicated, may hold values from -0.125 to 0.125
- light_out: bfloat16 [256, 2048], replicated, may hold values from -0.375 to 0.375
- heavy_query: bfloat16 [2048, 1024], P(None, 'head'), may hold values from -0.1875 to 0.1875
- heavy_key: bfloat16 [2048, 1024], P(None, 'head'), may hold values from -0.1875 to 0.1875
- heavy_value: bfloat16 [2048, 1024], P(None, 'head'), may hold values from -0.125 to 0.125
- heavy_out: bfloat16 [1024, 2048], P('head'), may hold values from -0.1875 to 0.1875
Outputs:
- layer_out: bfloat16 [131072, 2048], P(('seq', 'head'))
The draws below stay inside these ranges and needn't reach their ends.
Inputs may be any that keep to these rules, and one draw needn't show every extreme that they name: `query_index`: ascending and distinct token positions; at most 512 of them lie in one block of 2048 tokens starting at a multiple of 2048, and some block holds exactly 512. `key_index`: ascending and distinct token positions; at most 192 of them lie in one block of 2048 tokens starting at a multiple of 2048, and some block holds exactly 192.
All inputs are finite; a program needn't handle non-finite values.
Results may differ from the reference program's by a relative error of at most 0.02.
Values may be sent and summed in bfloat16 or wider, within the bound.
No kernel may reach another device: no remote copies, remote signals or barrier semaphores. Data moves between devices by JAX's collectives and lax.ppermute only.
A program may use at most 128 MiB of HBM per device.

```python
import math
import jax
import jax.numpy as jnp
from jax import lax

D = 2048
HDIM = 64
LHEADS = 4
HHEADS = 16
RADIUS = 127
BLOCK = 2048
NBLK = 64
TOKENS = 131072
QROUTE = 8192
KROUTE = 8192
QCAP = 512
KCAP = 192


def routed_positions(key, total, most, low_weight, high_weight):
    first_key, second_key, third_key = jax.random.split(key, 3)
    block_ids = jnp.arange(NBLK, dtype=jnp.int32)
    hot_block = jax.random.randint(first_key, (), 0, NBLK, dtype=jnp.int32)
    is_hot = block_ids == hot_block
    weights_int = jax.random.randint(second_key, (NBLK,), low_weight, high_weight + 1, dtype=jnp.int32)
    weights_int = jnp.where(is_hot, 0, weights_int)
    remaining = total - most
    shares = remaining * weights_int // jnp.sum(weights_int)
    leftover = remaining - jnp.sum(shares)
    others_rank = jnp.cumsum(jnp.where(is_hot, 0, 1)) - 1
    shares = shares + jnp.where(~is_hot & (others_rank < leftover), 1, 0)
    counts = jnp.where(is_hot, most, shares).astype(jnp.int32)
    shuffled = jax.random.permutation(third_key, NBLK * BLOCK).astype(jnp.int32).reshape(NBLK, BLOCK)
    ranking = jnp.argsort(jnp.argsort(shuffled, axis=1, stable=True), axis=1, stable=True)
    chosen = (ranking < counts[:, None]).reshape(NBLK * BLOCK)
    return jnp.nonzero(chosen, size=total)[0].astype(jnp.int32)


def draw_query_index(key, part):
    return routed_positions(jax.random.fold_in(key, 11), QROUTE, QCAP, 2, 5)


def draw_key_index(key, part):
    return routed_positions(jax.random.fold_in(key, 23), KROUTE, KCAP, 4, 5)


def draw_tokens(key, part):
    first_key = jax.random.fold_in(jax.random.fold_in(key, 37), 0)
    entries = jax.random.truncated_normal(first_key, -5.0, 5.0, (TOKENS, D), jnp.float32)
    return entries.astype(jnp.bfloat16)


def block_levels(rng, extent, shards, least, top_value):
    level, own = 1.0, jax.random.fold_in(rng, 6)
    for dim, shards_of in shards:
        draws = jnp.exp(jax.random.uniform(jax.random.fold_in(own, dim), (shards_of,), jnp.float32, least / len(shards), top_value / len(shards)))
        level = level * jnp.repeat(draws, extent[dim] // shards_of).reshape([-1 if axis == dim else 1 for axis in range(len(extent))])
    return level


def noise(stream_key, shape, width, most, pieces=(), held_as=jnp.bfloat16):
    loudness = block_levels(stream_key, shape, pieces, -0.22, 0.18) if pieces else 1.0
    result = jax.random.normal(stream_key, shape, jnp.float32) * width * loudness
    return jnp.minimum(jnp.maximum(result, -most), most).astype(held_as)


def setup_inputs(seed: int = 0) -> dict:
    streams_of = jax.random.split(jax.random.key(seed), 12)
    tokens = draw_tokens(jax.random.fold_in(streams_of[11], 71), 0)
    query_index = draw_query_index(jax.random.fold_in(streams_of[11], 71), 0)
    key_index = draw_key_index(jax.random.fold_in(streams_of[11], 71), 0)
    light_query = noise(streams_of[3], (D, LHEADS * HDIM), (4 * D // 9) ** -0.5, 0.1875)
    light_key = noise(streams_of[4], (D, LHEADS * HDIM), (4 * D // 9) ** -0.5, 0.1875)
    light_value = noise(streams_of[5], (D, LHEADS * HDIM), D ** -0.5, 0.125)
    light_out = noise(streams_of[6], (LHEADS * HDIM, D), (LHEADS * HDIM) ** -0.5, 0.375)
    heavy_query = noise(streams_of[7], (D, HHEADS * HDIM), (4 * D // 9) ** -0.5, 0.1875, ((1, 4),))
    heavy_key = noise(streams_of[8], (D, HHEADS * HDIM), (4 * D // 9) ** -0.5, 0.1875, ((1, 4),))
    heavy_value = noise(streams_of[9], (D, HHEADS * HDIM), D ** -0.5, 0.125, ((1, 4),))
    heavy_out = noise(streams_of[10], (HHEADS * HDIM, D), (HHEADS * HDIM) ** -0.5, 0.1875, ((0, 4),))
    return dict(tokens=tokens, query_index=query_index, key_index=key_index, light_query=light_query, light_key=light_key, light_value=light_value, light_out=light_out, heavy_query=heavy_query, heavy_key=heavy_key, heavy_value=heavy_value, heavy_out=heavy_out)


def attend_rows(query_rows, key_rows, value_rows, allowed, head_count):
    row_count = query_rows.shape[0]
    key_count = key_rows.shape[0]
    head_dim = query_rows.shape[1] // head_count
    query_split = query_rows.astype(jnp.float32).reshape(row_count, head_count, head_dim)
    key_split = key_rows.astype(jnp.float32).reshape(key_count, head_count, head_dim)
    value_split = value_rows.astype(jnp.float32).reshape(key_count, head_count, head_dim)
    scores = jnp.einsum("qhd,khd->hqk", query_split, key_split) * (head_dim ** -0.5)
    scores = jnp.where(allowed[None], scores, -1e30)
    row_peak = jnp.max(scores, axis=2, keepdims=True)
    weights = jnp.where(allowed[None], jnp.exp(scores - row_peak), 0.0)
    row_total = jnp.sum(weights, axis=2)
    rounded = lax.optimization_barrier(weights.astype(jnp.bfloat16)).astype(jnp.float32)
    blended = jnp.einsum("hqk,khd->hqd", rounded, value_split) / row_total[:, :, None]
    blended = jnp.transpose(blended, (1, 0, 2)).reshape(row_count, head_count * head_dim)
    return blended.astype(jnp.bfloat16)


def project(rows_in, matrix):
    return jnp.dot(rows_in, matrix, preferred_element_type=jnp.float32).astype(jnp.bfloat16)


def reference(tokens, query_index, key_index, light_query, light_key, light_value, light_out, heavy_query, heavy_key, heavy_value, heavy_out):
    routed_q = project(tokens[query_index], heavy_query)
    routed_k = project(tokens[key_index], heavy_key)
    routed_v = project(tokens[key_index], heavy_value)
    every_key = jnp.ones((1, routed_k.shape[0]), dtype=bool)

    def one_head(head_number):
        start = head_number * HDIM
        return attend_rows(lax.dynamic_slice_in_dim(routed_q, start, HDIM, 1), lax.dynamic_slice_in_dim(routed_k, start, HDIM, 1), lax.dynamic_slice_in_dim(routed_v, start, HDIM, 1), every_key, 1)

    per_head = lax.map(one_head, jnp.arange(HHEADS, dtype=jnp.int32))
    heavy_mixed = jnp.transpose(per_head, (1, 0, 2)).reshape(routed_q.shape[0], HHEADS * HDIM)
    heavy_term = jnp.dot(heavy_mixed, heavy_out, preferred_element_type=jnp.float32)

    light_q_rows = project(tokens, light_query)
    light_k_rows = project(tokens, light_key)
    light_v_rows = project(tokens, light_value)
    margin = jnp.zeros((RADIUS, light_k_rows.shape[1]), jnp.bfloat16)
    key_padded = jnp.concatenate([margin, light_k_rows, margin], axis=0)
    value_padded = jnp.concatenate([margin, light_v_rows, margin], axis=0)
    span = math.gcd(TOKENS, 512)
    block_total = TOKENS // span

    def one_block(block_number):
        first = block_number * span
        query_rows = lax.dynamic_slice_in_dim(light_q_rows, first, span, 0)
        key_rows = lax.dynamic_slice_in_dim(key_padded, first, span + 2 * RADIUS, 0)
        value_rows = lax.dynamic_slice_in_dim(value_padded, first, span + 2 * RADIUS, 0)
        query_pos = first + jnp.arange(span, dtype=jnp.int32)
        key_pos = first - RADIUS + jnp.arange(span + 2 * RADIUS, dtype=jnp.int32)
        allowed = (jnp.abs(query_pos[:, None] - key_pos[None, :]) <= RADIUS) & (key_pos[None, :] >= 0) & (key_pos[None, :] < TOKENS)
        light_mixed = attend_rows(query_rows, key_rows, value_rows, allowed, LHEADS)
        light_term = jnp.dot(light_mixed, light_out, preferred_element_type=jnp.float32)
        slot = query_index - first
        slot = jnp.where((slot >= 0) & (slot < span), slot, span).astype(jnp.int32)
        heavy_part = jnp.zeros((span, D), jnp.float32).at[slot].add(heavy_term, mode="drop")
        return (light_term + heavy_part).astype(jnp.bfloat16)

    blocks = lax.map(one_block, jnp.arange(block_total, dtype=jnp.int32))
    return blocks.reshape(TOKENS, D)
```

```python
import functools

import jax
import jax.numpy as jnp
from jax import lax
from jax.experimental import pallas as pl
from jax.experimental.pallas import tpu as pltpu
from jax.sharding import Mesh
from jax.sharding import PartitionSpec as P

HDIM = 64
RADIUS = 127
HALO = 128
BLOCK_AXES = ("y", "z", "c")
ALL_AXES = ("y", "z", "c", "x")
LOW = -1e30
QTILE = 256
KCHUNK = 1024
Z_STEPS = (0, -1, 1, -2, 2, -3, 3, -4)


def shift(value, axis, distance):
    size = lax.axis_size(axis)
    return lax.ppermute(value, axis, [(i, (i + distance) % size) for i in range(size)])


def vmem():
    return pl.BlockSpec(memory_space=pltpu.VMEM)


def smem():
    return pl.BlockSpec(memory_space=pltpu.SMEM)


def cost(flops, moved, exps=0):
    return pl.CostEstimate(flops=flops, bytes_accessed=moved, transcendentals=exps)


def gather_weights(shard):
    half_rows = shard.shape[0] // 2
    quarter = half_rows // 2
    core = lax.axis_index("c")
    mine = lax.dynamic_slice_in_dim(shard, core * half_rows, half_rows, 0)
    theirs = lax.dynamic_slice_in_dim(shard, (1 - core) * half_rows, half_rows, 0)
    left = shift(mine, "x", 1)
    right = shift(mine, "x", -1)
    far = jnp.concatenate(
        [shift(left[:quarter], "x", 1), shift(right[quarter:], "x", -1)], axis=0
    )
    near = jnp.stack([left, right, far])
    other = shift(near, "c", 1)
    return mine, theirs, near, other


def light_kernel(first_ref, q_ref, prev_ref, own_ref, next_ref, out_ref, *, total):
    width = q_ref.shape[1]
    rows = q_ref.shape[0]
    tile = 2 * HALO
    span = tile + 2 * HALO
    padded = jnp.concatenate([prev_ref[...], own_ref[...], next_ref[...]], axis=0)
    row = lax.broadcasted_iota(jnp.int32, (tile, span), 0)
    col = lax.broadcasted_iota(jnp.int32, (tile, span), 1)
    near = jnp.abs(col - HALO - row) <= RADIUS
    for start in range(0, rows, tile):
        position = first_ref[0] + start - HALO + col
        allowed = near & (position >= 0) & (position < total)
        parts = []
        for head in range(width // HDIM):
            cols = slice(head * HDIM, (head + 1) * HDIM)
            keys = padded[start : start + span, cols]
            values = padded[start : start + span, width + head * HDIM : width + (head + 1) * HDIM]
            scores = lax.dot_general(
                q_ref[start : start + tile, cols],
                keys,
                (((1,), (1,)), ((), ())),
                preferred_element_type=jnp.float32,
            ) * (HDIM**-0.5)
            scores = jnp.where(allowed, scores, LOW)
            weights = jnp.exp(scores - jnp.max(scores, axis=1, keepdims=True))
            totals = jnp.sum(weights, axis=1, keepdims=True)
            mixed = jnp.dot(
                weights.astype(jnp.bfloat16), values, preferred_element_type=jnp.float32
            )
            parts.append(mixed / totals)
        out_ref[start : start + tile, :] = jnp.concatenate(parts, axis=1).astype(jnp.bfloat16)


def pair_kernel(place_ref, own_ref, a_ref, b_ref, c_ref, key_ref, value_ref, out_ref):
    rows = jnp.concatenate([own_ref[...], a_ref[...], b_ref[...], c_ref[...]], axis=0)
    keys = jnp.dot(rows, key_ref[...], preferred_element_type=jnp.float32).astype(jnp.bfloat16)
    values = jnp.dot(rows, value_ref[...], preferred_element_type=jnp.float32).astype(jnp.bfloat16)
    heads = out_ref.shape[0]
    for head in range(heads):
        cols = slice(head * HDIM, (head + 1) * HDIM)
        slot = (head - place_ref[0] + heads) % heads
        out_ref[slot] = jnp.concatenate([keys[:, cols], values[:, cols]], axis=1)


def query_kernel(place_ref, own_ref, a_ref, b_ref, c_ref, out_ref):
    rows = own_ref[...] + a_ref[...] + b_ref[...] + c_ref[...]
    heads = out_ref.shape[0]
    half = rows.shape[0] // 2
    for head in range(heads):
        cols = slice(head * HDIM, (head + 1) * HDIM)
        slot = (head - place_ref[0] + heads) % heads
        out_ref[slot] = jnp.concatenate([rows[:half, cols], rows[half:, cols]], axis=1)


def attention_kernel(
    place_ref,
    query_starts_ref,
    key_starts_ref,
    q0_ref,
    q1_ref,
    q2_ref,
    q3_ref,
    near_ref,
    far_ref,
    out_ref,
    queries,
    keys,
    values,
    results,
    *,
    sizes,
):
    y_size, z_size = sizes
    py, pz, pc, px = place_ref[0], place_ref[1], place_ref[2], place_ref[3]
    group = out_ref.shape[0]
    half = out_ref.shape[1]
    cap = 2 * half
    key_cap = near_ref.shape[0] // (y_size * z_size)
    quarter = key_cap // 4

    def block_of(rel_y, step_z, swap):
        by = (py - rel_y + y_size) % y_size
        bz = (pz + step_z + z_size) % z_size
        bc = (pc + swap) % 2
        return (by * z_size + bz) * 2 + bc

    lane = lax.broadcasted_iota(jnp.int32, (key_cap, 2 * HDIM), 1)
    row = lax.broadcasted_iota(jnp.int32, (key_cap, 2 * HDIM), 0)
    slot_ids = (row + (4 - 0) * 0)
    piece = row // quarter
    slot_ids = ((px - piece + 4) % 4) * quarter + (row - piece * quarter)
    low = jnp.full((key_cap, 2 * HDIM), LOW, jnp.bfloat16)
    zero = jnp.zeros((key_cap, 2 * HDIM), jnp.bfloat16)
    one = jnp.ones((key_cap, 2 * HDIM), jnp.bfloat16)
    for swap, source in ((0, near_ref), (1, far_ref)):
        for step, step_z in enumerate(Z_STEPS):
            for rel in range(y_size):
                block = block_of(rel, step_z, swap)
                count = key_starts_ref[block + 1] - key_starts_ref[block]
                valid = slot_ids < count
                start = (step * y_size + rel) * key_cap
                pair = source[start : start + key_cap, :]
                base = swap * near_ref.shape[0] + start
                keys[base : base + key_cap, :] = jnp.where(
                    lane < HDIM, pair, jnp.where((lane == HDIM) & ~valid, low, zero)
                )
                values[base : base + key_cap, :] = jnp.where(
                    lane >= HDIM, pair, jnp.where((lane == 0) & valid, one, zero)
                )

    queries[...] = jnp.zeros_like(queries)
    results[...] = jnp.zeros_like(results)
    q_lane = lax.broadcasted_iota(jnp.int32, (half, 2 * HDIM), 1)
    offsets = []
    offset = 0
    for rel, source in enumerate((q0_ref, q1_ref, q2_ref, q3_ref)):
        block = block_of(rel, 0, 0)
        count = query_starts_ref[block + 1] - query_starts_ref[block]
        offsets.append(offset)
        packed = source[...].astype(jnp.float32) * (HDIM**-0.5)
        rolled = pltpu.roll(packed, HDIM, 1)
        for number, value in ((0, packed), (1, rolled)):
            filled = jnp.where(q_lane < HDIM, value, jnp.where(q_lane == HDIM, 1.0, 0.0))
            queries[pl.ds(pl.multiple_of(offset + number * half, 16), half), :] = filled.astype(
                jnp.bfloat16
            )
        offset = offset + (count + 15) // 16 * 16

    def tile_step(tile, unused):
        rows = pl.ds(pl.multiple_of(tile * QTILE, QTILE), QTILE)
        q = queries[rows, :]

        def chunk_step(chunk, state):
            peak, acc = state
            span = pl.ds(pl.multiple_of(chunk * KCHUNK, KCHUNK), KCHUNK)
            scores = lax.dot_general(
                q, keys[span, :], (((1,), (1,)), ((), ())), preferred_element_type=jnp.float32
            )
            new_peak = jnp.maximum(peak, jnp.max(scores, axis=1, keepdims=True))
            weights = jnp.exp(scores - new_peak).astype(jnp.bfloat16)
            acc = acc * jnp.exp(peak - new_peak) + jnp.dot(
                weights, values[span, :], preferred_element_type=jnp.float32
            )
            return new_peak, acc

        peak, acc = lax.fori_loop(
            0,
            keys.shape[0] // KCHUNK,
            chunk_step,
            (
                jnp.full((QTILE, 1), LOW, jnp.float32),
                jnp.zeros((QTILE, 2 * HDIM), jnp.float32),
            ),
        )
        results[rows, :] = (acc / acc[:, 0:1]).astype(jnp.bfloat16)
        return unused

    lax.fori_loop(0, (offset + QTILE - 1) // QTILE, tile_step, 0)

    for rel in range(group):
        first = results[pl.ds(pl.multiple_of(offsets[rel], 16), half), :]
        second = results[pl.ds(pl.multiple_of(offsets[rel] + half, 16), half), :]
        out_ref[rel] = jnp.concatenate([first[:, HDIM:], second[:, HDIM:]], axis=1)


def final_kernel(
    place_ref,
    slots_ref,
    light_ref,
    light_out_ref,
    m0_ref,
    m1_ref,
    m2_ref,
    m3_ref,
    mine_ref,
    theirs_ref,
    near_ref,
    other_ref,
    out_ref,
    mixed,
):
    py, pc = place_ref[0], place_ref[2]
    rows = light_ref.shape[0]
    heads = m0_ref.shape[0]

    @pl.when(pl.program_id(0) == 0)
    def _():
        slots = slots_ref.shape[1]
        token = lax.broadcasted_iota(jnp.int32, (rows, slots), 0)
        place = jnp.where(token == slots_ref[...], 1.0, 0.0).astype(jnp.bfloat16)
        for number, source in enumerate((m0_ref, m1_ref, m2_ref, m3_ref)):
            parts = []
            for position in range(heads):
                head = (position + 2 * pc) % heads
                packed = source[(head - py + heads) % heads]
                parts.append(jnp.concatenate([packed[:, :HDIM], packed[:, HDIM:]], axis=0))
            wide = jnp.concatenate(parts, axis=1)
            mixed[number] = jnp.dot(place, wide, preferred_element_type=jnp.float32).astype(
                jnp.bfloat16
            )

    acc = jnp.dot(light_ref[...], light_out_ref[...], preferred_element_type=jnp.float32)
    for number in range(4):
        if number == 0:
            weights = jnp.concatenate([mine_ref[...], theirs_ref[...]], axis=0)
        else:
            weights = jnp.concatenate([near_ref[number - 1], other_ref[number - 1]], axis=0)
        acc += jnp.dot(mixed[number], weights, preferred_element_type=jnp.float32)
    out_ref[...] = acc.astype(out_ref.dtype)


def shards(
    tokens,
    query_index,
    key_index,
    light_query,
    light_key,
    light_value,
    light_out,
    heavy_query,
    heavy_key,
    heavy_value,
    heavy_out,
):
    rows, model = tokens.shape
    y_size, z_size, x_size = lax.axis_size("y"), lax.axis_size("z"), lax.axis_size("x")
    blocks = y_size * z_size * 2
    block_len = rows * x_size
    py, pz, pc, px = (lax.axis_index(a) for a in ALL_AXES)
    block = (py * z_size + pz) * 2 + pc
    first = (block * x_size + px) * rows
    query_cap = block_len // 4
    key_cap = 3 * block_len // 32
    quarter = key_cap // x_size
    width = light_query.shape[1]
    heavy_width = heavy_query.shape[1]
    bf16, f32 = jnp.bfloat16, jnp.float32
    place = jnp.stack([py, pz, pc, px]).astype(jnp.int32)

    bounds = jnp.arange(blocks + 1, dtype=jnp.int32) * block_len
    key_starts = jnp.sum((key_index[None, :] < bounds[:, None]).astype(jnp.int32), axis=1)
    query_starts = jnp.sum((query_index[None, :] < bounds[:, None]).astype(jnp.int32), axis=1)
    key_begin = jnp.sum((key_index < block * block_len).astype(jnp.int32))
    query_begin = jnp.sum((query_index < block * block_len).astype(jnp.int32))

    key_list = jnp.concatenate([key_index, jnp.full((key_cap,), -1, jnp.int32)])
    key_slots = lax.dynamic_slice_in_dim(key_list, key_begin, key_cap, 0) - first
    token_ids = jnp.arange(rows, dtype=jnp.int32)
    key_hot = (key_slots[:, None] == token_ids[None, :]).astype(bf16)
    picked = jnp.dot(key_hot, tokens, preferred_element_type=f32).astype(bf16)
    picked = picked.reshape(x_size, quarter, model)
    piece = lax.dynamic_index_in_dim(picked, px, 0, keepdims=False)
    for step in (1, -1, 2):
        sent = lax.dynamic_index_in_dim(picked, (px + step) % x_size, 0, keepdims=False)
        piece = piece + shift(sent, "x", step)
    row_pieces = [piece] + [shift(piece, "x", step) for step in (1, 2, 3)]

    light_rows = jnp.dot(tokens, light_query, preferred_element_type=f32).astype(bf16)
    light_pair = jnp.concatenate(
        [
            jnp.dot(tokens, light_key, preferred_element_type=f32).astype(bf16),
            jnp.dot(tokens, light_value, preferred_element_type=f32).astype(bf16),
        ],
        axis=1,
    )
    devices = blocks * x_size
    up = [(i, i + 1) for i in range(devices - 1)]
    before = lax.ppermute(light_pair[rows - HALO :], ALL_AXES, up)
    after = lax.ppermute(light_pair[:HALO], ALL_AXES, [(b, a) for a, b in up])
    light_mixed = pl.pallas_call(
        functools.partial(light_kernel, total=rows * devices),
        out_shape=jax.ShapeDtypeStruct((rows, width), bf16),
        in_specs=[smem()] + [vmem()] * 4,
        out_specs=vmem(),
        cost_estimate=cost(4 * rows * 512 * 256 * 4, 4 * rows * width * 2, 4 * rows * 512),
        name="light",
    )(first.reshape(1), light_rows, before, light_pair, after)

    query_list = jnp.concatenate([query_index, jnp.full((query_cap,), -1, jnp.int32)])
    query_slots = lax.dynamic_slice_in_dim(query_list, query_begin, query_cap, 0) - first
    query_hot = (query_slots[:, None] == token_ids[None, :]).astype(bf16)
    q_mine, q_theirs, q_near, q_other = gather_weights(heavy_query)
    half = model // 2
    chosen = []
    for core in (pc, 1 - pc):
        part = lax.dynamic_slice_in_dim(tokens, core * half, half, 1)
        chosen.append(jnp.dot(query_hot, part, preferred_element_type=f32).astype(bf16))

    def project(a, b):
        return (
            jnp.dot(chosen[0], a, preferred_element_type=f32)
            + jnp.dot(chosen[1], b, preferred_element_type=f32)
        ).astype(bf16)

    q_own = project(q_mine, q_theirs)
    q_in = [
        shift(project(q_near[i], q_other[i]), "x", step) for i, step in enumerate((-1, 1, 2))
    ]
    q_heads = pl.pallas_call(
        query_kernel,
        out_shape=jax.ShapeDtypeStruct((y_size, query_cap // 2, 2 * HDIM), bf16),
        in_specs=[smem()] + [vmem()] * 4,
        out_specs=vmem(),
        cost_estimate=cost(4 * query_cap * heavy_width, 10 * query_cap * heavy_width),
        name="query_heads",
    )(place, q_own, *q_in)
    q_mine_y = [q_heads[0]] + [shift(q_heads[r], "y", r) for r in range(1, y_size)]

    pair = pl.pallas_call(
        pair_kernel,
        out_shape=jax.ShapeDtypeStruct((y_size, key_cap, 2 * HDIM), bf16),
        in_specs=[smem()] + [vmem()] * 6,
        out_specs=vmem(),
        cost_estimate=cost(4 * key_cap * model * heavy_width, 4 * model * heavy_width),
        name="key_value_heads",
    )(place, *row_pieces, heavy_key, heavy_value)
    column = jnp.concatenate([pair[0]] + [shift(pair[r], "y", r) for r in range(1, y_size)], axis=0)
    ring = {0: column}
    for step in range(1, z_size // 2 + 1):
        ring[-step] = shift(ring[-step + 1], "z", 1)
        if step < z_size // 2:
            ring[step] = shift(ring[step - 1], "z", -1)
    near_pairs = jnp.concatenate([ring[s] for s in Z_STEPS], axis=0)
    far_pairs = shift(near_pairs, "c", 1)

    key_total = 2 * near_pairs.shape[0]
    slots_total = y_size * query_cap + QTILE
    heads_out = pl.pallas_call(
        functools.partial(attention_kernel, sizes=(y_size, z_size)),
        out_shape=jax.ShapeDtypeStruct((y_size, query_cap // 2, 2 * HDIM), bf16),
        in_specs=[smem()] * 3 + [vmem()] * 6,
        out_specs=vmem(),
        scratch_shapes=[
            pltpu.VMEM((slots_total, 2 * HDIM), bf16),
            pltpu.VMEM((key_total, 2 * HDIM), bf16),
            pltpu.VMEM((key_total, 2 * HDIM), bf16),
            pltpu.VMEM((slots_total, 2 * HDIM), bf16),
        ],
        cost_estimate=cost(
            4 * 1024 * key_total * 256, 4 * key_total * HDIM * 2, 1024 * key_total
        ),
        name="heavy_attention",
    )(place, query_starts, key_starts, *q_mine_y, near_pairs, far_pairs)

    back = jnp.stack([heads_out[0]] + [shift(heads_out[r], "y", -r) for r in range(1, y_size)])
    o_mine, o_theirs, o_near, o_other = gather_weights(heavy_out)
    groups = [back] + [shift(back, "x", step) for step in (1, -1, 2)]
    column_tile = 512
    out = pl.pallas_call(
        final_kernel,
        grid=(model // column_tile,),
        out_shape=jax.ShapeDtypeStruct((rows, model), bf16),
        in_specs=[
            smem(),
            pl.BlockSpec((1, query_cap), lambda j: (0, 0)),
            pl.BlockSpec((rows, width), lambda j: (0, 0)),
            pl.BlockSpec((width, column_tile), lambda j: (0, j)),
        ]
        + [pl.BlockSpec((y_size, query_cap // 2, 2 * HDIM), lambda j: (0, 0, 0))] * 4
        + [pl.BlockSpec((heavy_width // 2, column_tile), lambda j: (0, j))] * 2
        + [pl.BlockSpec((3, heavy_width // 2, column_tile), lambda j: (0, 0, j))] * 2,
        out_specs=pl.BlockSpec((rows, column_tile), lambda j: (0, j)),
        scratch_shapes=[pltpu.VMEM((4, rows, heavy_width), bf16)],
        cost_estimate=cost(2 * rows * 1280 * model, 10 * rows * model),
        name="combine",
    )(
        place,
        query_slots.reshape(1, query_cap),
        light_mixed,
        light_out,
        *groups,
        o_mine,
        o_theirs,
        o_near,
        o_other,
    )
    return out


def solution(mesh):
    torus = Mesh(mesh.devices.reshape(4, 8, 2, mesh.shape["head"]), ALL_AXES)
    return jax.shard_map(
        shards,
        mesh=torus,
        in_specs=(P(ALL_AXES, None),)
        + (P(),) * 6
        + (P(None, "x"),) * 3
        + (P("x", None),),
        out_specs=P(ALL_AXES, None),
        check_vma=False,
    )
```

```python
import functools

import jax
import jax.numpy as jnp
from jax import lax
from jax.experimental import pallas as pl
from jax.experimental.pallas import tpu as pltpu
from jax.sharding import Mesh
from jax.sharding import PartitionSpec as P


HDIM = 64
RADIUS = 127
HALO = 128
ALL_AXES = ("y", "z", "c", "x")
LOW = -1e30
QTILE = 512
KCHUNK = 3072
Z_STEPS = (0, -1, 1, -2, 2, -3, 3, -4)


def shift(value, axis, distance):
    size = lax.axis_size(axis)
    return lax.ppermute(value, axis, [(i, (i + distance) % size) for i in range(size)])


def opposite(value):
    size = lax.axis_size("x")
    pairs = [(i, (i + 1) % size) for i in range(size)]
    pairs += [(size + i, size + (i - 1) % size) for i in range(size)]
    return lax.ppermute(value, ("c", "x"), pairs)


def gather_weights(shard):
    near = opposite(shard)
    half = shard.shape[0] // 2
    far = opposite(lax.dynamic_slice_in_dim(near, lax.axis_index("c") * half, half, 0))
    return (near, shift(near, "c", 1), far, shift(far, "c", 1))


def vmem():
    return pl.BlockSpec(memory_space=pltpu.VMEM)


def smem():
    return pl.BlockSpec(memory_space=pltpu.SMEM)


def cost(flops, moved, exps=0):
    return pl.CostEstimate(flops=flops, bytes_accessed=moved, transcendentals=exps)


def light_kernel(first_ref, q_ref, prev_ref, own_ref, next_ref, out_ref, *, total):
    width = q_ref.shape[1]
    rows = q_ref.shape[0]
    tile = 2 * HALO
    span = tile + 2 * HALO
    padded = jnp.concatenate([prev_ref[...], own_ref[...], next_ref[...]], axis=0)
    row = lax.broadcasted_iota(jnp.int32, (tile, span), 0)
    col = lax.broadcasted_iota(jnp.int32, (tile, span), 1)
    near = jnp.abs(col - HALO - row) <= RADIUS
    for start in range(0, rows, tile):
        position = first_ref[0] + start - HALO + col
        allowed = near & (position >= 0) & (position < total)
        parts = []
        for head in range(width // HDIM):
            cols = slice(head * HDIM, (head + 1) * HDIM)
            keys = padded[start : start + span, cols]
            values = padded[start : start + span, width + head * HDIM : width + (head + 1) * HDIM]
            scores = lax.dot_general(
                q_ref[start : start + tile, cols],
                keys,
                (((1,), (1,)), ((), ())),
                preferred_element_type=jnp.float32,
            ) * (HDIM**-0.5)
            scores = jnp.where(allowed, scores, LOW)
            weights = jnp.exp(scores - jnp.max(scores, axis=1, keepdims=True))
            totals = jnp.sum(weights, axis=1, keepdims=True)
            mixed = jnp.dot(
                weights.astype(jnp.bfloat16), values, preferred_element_type=jnp.float32
            )
            parts.append(mixed / totals)
        out_ref[start : start + tile, :] = jnp.concatenate(parts, axis=1).astype(jnp.bfloat16)


def pick_kernel(place_ref, slots_ref, tokens_ref, *out_refs):
    groups = len(out_refs)
    quarter = out_refs[0].shape[0]
    tokens = tokens_ref[...]
    token = lax.broadcasted_iota(jnp.int32, (quarter, tokens.shape[0]), 1)
    hots = []
    for step in range(groups):
        group = (place_ref[3] + step) % groups
        slots = slots_ref[pl.ds(pl.multiple_of(group * quarter, 16), quarter), :]
        hots.append(jnp.where(token == slots, 1.0, 0.0).astype(jnp.bfloat16))
    picked = jnp.dot(
        jnp.concatenate(hots, axis=0), tokens, preferred_element_type=jnp.float32
    ).astype(jnp.bfloat16)
    for step in range(groups):
        out_refs[step][...] = picked[step * quarter : (step + 1) * quarter]


def local_kernel(
    tokens_ref, query_ref, key_ref, value_ref, q_ref, pair_ref, head_ref, tail_ref
):
    tokens = tokens_ref[...]
    rows = tokens.shape[0]
    width = query_ref.shape[1]
    q_ref[...] = jnp.dot(tokens, query_ref[...], preferred_element_type=jnp.float32).astype(
        jnp.bfloat16
    )
    for number, weights in enumerate((key_ref, value_ref)):
        part = jnp.dot(tokens, weights[...], preferred_element_type=jnp.float32).astype(
            jnp.bfloat16
        )
        cols = slice(number * width, (number + 1) * width)
        pair_ref[:, cols] = part
        head_ref[:, cols] = part[:HALO]
        tail_ref[:, cols] = part[rows - HALO :]


def select_kernel(slots_ref, tokens_ref, out_ref):
    slots = slots_ref.shape[0]
    token = lax.broadcasted_iota(jnp.int32, (slots, tokens_ref.shape[0]), 1)
    hot = jnp.where(token == slots_ref[...], 1.0, 0.0).astype(jnp.bfloat16)
    out_ref[...] = jnp.dot(hot, tokens_ref[...], preferred_element_type=jnp.float32).astype(
        jnp.bfloat16
    )


def project_kernel(place_ref, rows_ref, own_ref, near_ref, near2_ref, far_ref, far2_ref, *refs):
    outs, far = refs[:-1], refs[-1]
    core = place_ref[2]
    half = far_ref.shape[0]
    far[pl.ds(pl.multiple_of(core * half, half), half), :] = far_ref[...]
    far[pl.ds(pl.multiple_of((1 - core) * half, half), half), :] = far2_ref[...]
    rows = rows_ref[...]

    def times(weights):
        return jnp.dot(rows, weights, preferred_element_type=jnp.float32).astype(jnp.bfloat16)

    outs[0][...] = times(own_ref[...])
    outs[3][...] = times(far[...])

    @pl.when(core == 0)
    def _():
        outs[1][...] = times(near_ref[...])
        outs[2][...] = times(near2_ref[...])

    @pl.when(core == 1)
    def _():
        outs[1][...] = times(near2_ref[...])
        outs[2][...] = times(near_ref[...])


def pair_kernel(place_ref, own_ref, a_ref, b_ref, c_ref, key_ref, value_ref, *refs):
    outs, rows, heads_scratch = refs[:-2], refs[-2], refs[-1]
    quarter = own_ref.shape[0]
    for number, source in enumerate((own_ref, a_ref, b_ref, c_ref)):
        group = (place_ref[3] - number + 4) % 4
        rows[pl.ds(pl.multiple_of(group * quarter, 16), quarter), :] = source[...]
    every = rows[...]
    keys = jnp.dot(every, key_ref[...], preferred_element_type=jnp.float32).astype(jnp.bfloat16)
    values = jnp.dot(every, value_ref[...], preferred_element_type=jnp.float32).astype(
        jnp.bfloat16
    )
    heads = len(outs)
    for head in range(heads):
        cols = slice(head * HDIM, (head + 1) * HDIM)
        slot = (head - place_ref[0] + heads) % heads
        heads_scratch[slot] = jnp.concatenate([keys[:, cols], values[:, cols]], axis=1)
    for slot in range(heads):
        outs[slot][...] = heads_scratch[slot]


def query_kernel(place_ref, own_ref, a_ref, b_ref, c_ref, *refs):
    outs, heads_scratch = refs[:-1], refs[-1]
    rows = own_ref[...] + a_ref[...] + b_ref[...] + c_ref[...]
    heads = len(outs)
    half = rows.shape[0] // 2
    for head in range(heads):
        cols = slice(head * HDIM, (head + 1) * HDIM)
        slot = (head - place_ref[0] + heads) % heads
        heads_scratch[slot] = jnp.concatenate([rows[:half, cols], rows[half:, cols]], axis=1)
    for slot in range(heads):
        outs[slot][...] = heads_scratch[slot]


def stack_kernel(*refs):
    *sources, out_ref = refs
    size = sources[0].shape[0]
    for number, source in enumerate(sources):
        out_ref[number * size : (number + 1) * size, :] = source[...]


def stack_rows(*pieces):
    size, width = pieces[0].shape
    return pl.pallas_call(
        stack_kernel,
        out_shape=jax.ShapeDtypeStruct((len(pieces) * size, width), pieces[0].dtype),
        in_specs=[vmem()] * len(pieces),
        out_specs=vmem(),
        cost_estimate=cost(0, 4 * len(pieces) * size * width),
    )(*pieces)


def attention_kernel(place_ref, query_starts_ref, key_starts_ref, *refs, sizes):
    y_size, z_size = sizes
    q_refs, refs = refs[:y_size], refs[y_size:]
    near_refs, refs = refs[:z_size], refs[z_size:]
    far_refs, refs = refs[:z_size], refs[z_size:]
    out_refs, refs = refs[:y_size], refs[y_size:]
    queries, keys, values, results = refs
    py, pz, pc = place_ref[0], place_ref[1], place_ref[2]
    half = q_refs[0].shape[0]
    key_cap = near_refs[0].shape[0] // y_size

    def block_of(rel_y, step_z, swap):
        by = (py - rel_y + y_size) % y_size
        bz = (pz + step_z + z_size) % z_size
        bc = (pc + swap) % 2
        return (by * z_size + bz) * 2 + bc

    lane = lax.broadcasted_iota(jnp.int32, (key_cap, 2 * HDIM), 1)
    slot_ids = lax.broadcasted_iota(jnp.int32, (key_cap, 1), 0)
    total = 0
    for swap, sources in ((0, near_refs), (1, far_refs)):
        for step_z, source in zip(Z_STEPS, sources):

            def place_piece(rel, total, swap=swap, step_z=step_z, source=source):
                block = block_of(rel, step_z, swap)
                count = key_starts_ref[block + 1] - key_starts_ref[block]
                start = pl.multiple_of(rel * key_cap, 16)
                pair = source[pl.ds(start, key_cap), :].astype(jnp.float32)
                valid = slot_ids < count
                target = pl.ds(pl.multiple_of(total, 16), key_cap)
                keys[target, :] = jnp.where(
                    lane < HDIM,
                    pair,
                    jnp.where(lane == HDIM, jnp.where(valid, 0.0, LOW), 0.0),
                ).astype(jnp.bfloat16)
                values[target, :] = jnp.where(
                    lane >= HDIM,
                    pair,
                    jnp.where(lane == 0, jnp.where(valid, 1.0, 0.0), 0.0),
                ).astype(jnp.bfloat16)
                return total + (count + 15) // 16 * 16

            total = lax.fori_loop(0, y_size, place_piece, total)
    tail_lane = lax.broadcasted_iota(jnp.int32, (KCHUNK, 2 * HDIM), 1)
    tail = pl.ds(pl.multiple_of(total, 16), KCHUNK)
    keys[tail, :] = jnp.where(tail_lane == HDIM, LOW, 0.0).astype(jnp.bfloat16)
    values[tail, :] = jnp.zeros((KCHUNK, 2 * HDIM), jnp.bfloat16)

    queries[...] = jnp.zeros_like(queries)
    results[...] = jnp.zeros_like(results)
    q_lane = lax.broadcasted_iota(jnp.int32, (half, 2 * HDIM), 1)
    offsets = []
    offset = 0
    for rel, source in enumerate(q_refs):
        block = block_of(rel, 0, 0)
        count = query_starts_ref[block + 1] - query_starts_ref[block]
        offsets.append(offset)
        packed = source[...].astype(jnp.float32) * (HDIM**-0.5)
        rolled = pltpu.roll(packed, HDIM, 1)
        for number, value in ((0, packed), (1, rolled)):
            filled = jnp.where(q_lane < HDIM, value, jnp.where(q_lane == HDIM, 1.0, 0.0))
            queries[pl.ds(pl.multiple_of(offset + number * half, 16), half), :] = filled.astype(
                jnp.bfloat16
            )
        offset = offset + (count + 15) // 16 * 16
    chunks = (total + KCHUNK - 1) // KCHUNK

    def tile_step(tile, unused):
        rows = pl.ds(pl.multiple_of(tile * QTILE, QTILE), QTILE)
        q = queries[rows, :]

        def chunk_step(chunk, state):
            peak, acc = state
            span = pl.ds(pl.multiple_of(chunk * KCHUNK, KCHUNK), KCHUNK)
            scores = lax.dot_general(
                q, keys[span, :], (((1,), (1,)), ((), ())), preferred_element_type=jnp.float32
            )
            new_peak = jnp.maximum(peak, jnp.max(scores, axis=1, keepdims=True))
            weights = jnp.exp(scores - new_peak).astype(jnp.bfloat16)
            acc = acc * jnp.exp(peak - new_peak) + jnp.dot(
                weights, values[span, :], preferred_element_type=jnp.float32
            )
            return new_peak, acc

        _, acc = lax.fori_loop(
            0,
            chunks,
            chunk_step,
            (
                jnp.full((QTILE, 1), LOW, jnp.float32),
                jnp.zeros((QTILE, 2 * HDIM), jnp.float32),
            ),
        )
        results[rows, :] = (acc / acc[:, 0:1]).astype(jnp.bfloat16)
        return unused

    lax.fori_loop(0, (offset + QTILE - 1) // QTILE, tile_step, 0)

    for rel, out in enumerate(out_refs):
        first = results[pl.ds(pl.multiple_of(offsets[rel], 16), half), :]
        second = results[pl.ds(pl.multiple_of(offsets[rel] + half, 16), half), :]
        out[...] = jnp.concatenate([first[:, HDIM:], second[:, HDIM:]], axis=1)


def final_kernel(
    place_ref,
    slots_ref,
    light_ref,
    light_out_ref,
    m0_ref,
    m1_ref,
    m2_ref,
    m3_ref,
    own_ref,
    near_ref,
    near2_ref,
    far_ref,
    far2_ref,
    out_ref,
    mixed,
):
    py, pc = place_ref[0], place_ref[2]
    rows = light_ref.shape[0]
    heads = 4
    half = m0_ref.shape[0] // heads

    @pl.when(pl.program_id(0) == 0)
    def _():
        slots = slots_ref.shape[1]
        token = lax.broadcasted_iota(jnp.int32, (rows, slots), 0)
        place = jnp.where(token == slots_ref[...], 1.0, 0.0).astype(jnp.bfloat16)
        for number, source in enumerate((m0_ref, m1_ref, m2_ref, m3_ref)):
            parts = []
            for position in range(heads):
                head = (position + 2 * pc) % heads if number == 3 else position
                start = (head - py + heads) % heads * half
                packed = source[pl.ds(pl.multiple_of(start, half), half), :]
                parts.append(jnp.concatenate([packed[:, :HDIM], packed[:, HDIM:]], axis=0))
            wide = jnp.concatenate(parts, axis=1)
            mixed[number] = jnp.dot(place, wide, preferred_element_type=jnp.float32).astype(
                jnp.bfloat16
            )

    acc = jnp.dot(light_ref[...], light_out_ref[...], preferred_element_type=jnp.float32)
    acc += jnp.dot(mixed[0], own_ref[...], preferred_element_type=jnp.float32)
    acc += jnp.dot(mixed[1 + pc], near_ref[...], preferred_element_type=jnp.float32)
    acc += jnp.dot(mixed[2 - pc], near2_ref[...], preferred_element_type=jnp.float32)
    far = jnp.concatenate([far_ref[...], far2_ref[...]], axis=0)
    acc += jnp.dot(mixed[3], far, preferred_element_type=jnp.float32)
    out_ref[...] = acc.astype(out_ref.dtype)


def layer(
    tokens,
    query_index,
    key_index,
    light_query,
    light_key,
    light_value,
    light_out,
    heavy_query,
    heavy_key,
    heavy_value,
    heavy_out,
):
    rows, model = tokens.shape
    y_size, z_size, x_size = lax.axis_size("y"), lax.axis_size("z"), lax.axis_size("x")
    blocks = y_size * z_size * 2
    block_len = rows * x_size
    py, pz, pc, px = (lax.axis_index(a) for a in ALL_AXES)
    block = (py * z_size + pz) * 2 + pc
    first = (block * x_size + px) * rows
    query_cap = block_len // 4
    key_cap = 3 * block_len // 32
    quarter = key_cap // x_size
    width = light_query.shape[1]
    heavy_width = heavy_query.shape[1]
    bf16 = jnp.bfloat16
    place = jnp.stack([py, pz, pc, px]).astype(jnp.int32)

    def array(*shape):
        return jax.ShapeDtypeStruct(shape, bf16)

    wq = gather_weights(heavy_query)

    key_begin = jnp.sum((key_index < block * block_len).astype(jnp.int32))
    key_list = jnp.concatenate([key_index, jnp.full((key_cap,), -1, jnp.int32)])
    key_slots = lax.dynamic_slice_in_dim(key_list, key_begin, key_cap, 0) - first
    picked = pl.pallas_call(
        pick_kernel,
        out_shape=[array(quarter, model)] * x_size,
        in_specs=[smem()] + [vmem()] * 2,
        out_specs=[vmem()] * x_size,
        cost_estimate=cost(2 * key_cap * rows * model, 2 * rows * model),
        name="pick",
    )(place, key_slots.reshape(key_cap, 1), tokens)
    arrived = [shift(picked[step], "x", step) for step in (1, 3, 2)]
    piece = picked[0] + arrived[0] + arrived[1] + arrived[2]
    row_pieces = [piece] + [shift(piece, "x", step) for step in (1, 2, 3)]

    light_rows, light_pair, head, tail = pl.pallas_call(
        local_kernel,
        out_shape=[array(rows, width), array(rows, 2 * width)] + [array(HALO, 2 * width)] * 2,
        in_specs=[vmem()] * 4,
        out_specs=[vmem()] * 4,
        cost_estimate=cost(6 * rows * width * model, 2 * rows * model + 6 * model * width),
        name="light_project",
    )(tokens, light_query, light_key, light_value)
    devices = blocks * x_size
    up = [(i, i + 1) for i in range(devices - 1)]
    before = lax.ppermute(tail, ALL_AXES, up)
    after = lax.ppermute(head, ALL_AXES, [(b, a) for a, b in up])
    light_mixed = pl.pallas_call(
        functools.partial(light_kernel, total=rows * devices),
        out_shape=array(rows, width),
        in_specs=[smem()] + [vmem()] * 4,
        out_specs=vmem(),
        cost_estimate=cost(4 * rows * 512 * 256 * 4, 4 * rows * width * 2, 4 * rows * 512),
        name="light",
    )(first.reshape(1), light_rows, before, light_pair, after)

    query_begin = jnp.sum((query_index < block * block_len).astype(jnp.int32))
    query_list = jnp.concatenate([query_index, jnp.full((query_cap,), -1, jnp.int32)])
    query_slots = lax.dynamic_slice_in_dim(query_list, query_begin, query_cap, 0) - first
    chosen = pl.pallas_call(
        select_kernel,
        out_shape=array(query_cap, model),
        in_specs=[vmem()] * 2,
        out_specs=vmem(),
        cost_estimate=cost(2 * query_cap * rows * model, 4 * rows * model),
        name="select",
    )(query_slots.reshape(query_cap, 1), tokens)
    bounds = jnp.arange(blocks + 1, dtype=jnp.int32) * block_len
    key_starts = jnp.sum((key_index[None, :] < bounds[:, None]).astype(jnp.int32), axis=1)
    query_starts = jnp.sum((query_index[None, :] < bounds[:, None]).astype(jnp.int32), axis=1)

    pairs = pl.pallas_call(
        pair_kernel,
        out_shape=[array(key_cap, 2 * HDIM)] * y_size,
        in_specs=[smem()] + [vmem()] * 6,
        out_specs=[vmem()] * y_size,
        scratch_shapes=[
            pltpu.VMEM((key_cap, model), bf16),
            pltpu.VMEM((y_size, key_cap, 2 * HDIM), bf16),
        ],
        cost_estimate=cost(4 * key_cap * model * heavy_width, 4 * model * heavy_width),
        name="key_value_heads",
    )(place, *row_pieces, heavy_key, heavy_value)
    column = stack_rows(pairs[0], *[shift(pairs[r], "y", r) for r in range(1, y_size)])

    projected = pl.pallas_call(
        project_kernel,
        out_shape=[array(query_cap, heavy_width)] * x_size,
        in_specs=[smem()] + [vmem()] * 6,
        out_specs=[vmem()] * x_size,
        scratch_shapes=[pltpu.VMEM((model, heavy_width), bf16)],
        cost_estimate=cost(8 * query_cap * model * heavy_width, 8 * model * heavy_width),
        name="query_project",
    )(place, chosen, heavy_query, *wq)
    q_in = [shift(projected[i + 1], "x", step) for i, step in enumerate((-1, 1, 2))]
    q_heads = pl.pallas_call(
        query_kernel,
        out_shape=[array(query_cap // 2, 2 * HDIM)] * y_size,
        in_specs=[smem()] + [vmem()] * 4,
        out_specs=[vmem()] * y_size,
        scratch_shapes=[pltpu.VMEM((y_size, query_cap // 2, 2 * HDIM), bf16)],
        cost_estimate=cost(4 * query_cap * heavy_width, 10 * query_cap * heavy_width),
        name="query_heads",
    )(place, projected[0], *q_in)
    q_column = [q_heads[0]] + [shift(q_heads[r], "y", r) for r in range(1, y_size)]

    wo = gather_weights(heavy_out)

    ring = {0: column}
    for step in range(1, z_size // 2 + 1):
        ring[-step] = shift(ring[-step + 1], "z", 1)
        if step < z_size // 2:
            ring[step] = shift(ring[step - 1], "z", -1)
    near_pairs = [ring[s] for s in Z_STEPS]
    far_pairs = [shift(ring[s], "c", 1) for s in Z_STEPS]

    key_total = 2 * z_size * column.shape[0]
    slots_total = y_size * query_cap + QTILE
    heads_out = pl.pallas_call(
        functools.partial(attention_kernel, sizes=(y_size, z_size)),
        out_shape=[array(query_cap // 2, 2 * HDIM)] * y_size,
        in_specs=[smem()] * 3 + [vmem()] * (y_size + 2 * z_size),
        out_specs=[vmem()] * y_size,
        scratch_shapes=[
            pltpu.VMEM((slots_total, 2 * HDIM), bf16),
            pltpu.VMEM((key_total + KCHUNK, 2 * HDIM), bf16),
            pltpu.VMEM((key_total + KCHUNK, 2 * HDIM), bf16),
            pltpu.VMEM((slots_total, 2 * HDIM), bf16),
        ],
        cost_estimate=cost(4 * 1024 * key_total * 256, 4 * key_total * HDIM, 1024 * key_total),
        name="heavy_attention",
    )(place, query_starts, key_starts, *q_column, *near_pairs, *far_pairs)

    back = stack_rows(heads_out[0], *[shift(heads_out[r], "y", -r) for r in range(1, y_size)])
    groups = [back] + [shift(back, "x", step) for step in (1, -1, 2)]
    tile = 512

    def whole(*shape):
        return pl.BlockSpec(shape, lambda j: (0,) * len(shape))

    def columns(count):
        return pl.BlockSpec((count, tile), lambda j: (0, j))

    return pl.pallas_call(
        final_kernel,
        grid=(model // tile,),
        out_shape=array(rows, model),
        in_specs=[smem(), whole(1, query_cap), whole(rows, width), columns(width)]
        + [whole(y_size * query_cap // 2, 2 * HDIM)] * 4
        + [columns(heavy_width)]
        + [columns(p.shape[0]) for p in wo],
        out_specs=columns(rows),
        scratch_shapes=[pltpu.VMEM((4, rows, heavy_width), bf16)],
        cost_estimate=cost(2 * rows * 1280 * model, 10 * rows * model),
        name="combine",
    )(
        place,
        query_slots.reshape(1, query_cap),
        light_mixed,
        light_out,
        *groups,
        heavy_out,
        *wo,
    )


def solution(mesh):
    torus = Mesh(mesh.devices.reshape(4, 8, 2, mesh.shape["head"]), ALL_AXES)
    return jax.shard_map(
        layer,
        mesh=torus,
        in_specs=(P(ALL_AXES, None),)
        + (P(),) * 6
        + (P(None, "x"),) * 3
        + (P("x", None),),
        out_specs=P(ALL_AXES, None),
        check_vma=False,
    )
```

```python
import functools

import jax
import jax.numpy as jnp
from jax import lax
from jax.experimental import pallas as pl
from jax.experimental.pallas import tpu as pltpu
from jax.sharding import Mesh
from jax.sharding import PartitionSpec as P


HDIM = 64
RADIUS = 127
HALO = 128
ALL_AXES = ("y", "z", "c", "x")
LOW = -1e30
QTILE = 512
KCHUNK = 3072
Z_STEPS = (0, -1, 1, -2, 2, -3, 3, -4)


def shift(value, axis, distance):
    size = lax.axis_size(axis)
    return lax.ppermute(value, axis, [(i, (i + distance) % size) for i in range(size)])


def opposite(value):
    size = lax.axis_size("x")
    pairs = [(i, (i + 1) % size) for i in range(size)]
    pairs += [(size + i, size + (i - 1) % size) for i in range(size)]
    return lax.ppermute(value, ("c", "x"), pairs)


def gather_weights(shard):
    near = opposite(shard)
    half = shard.shape[0] // 2
    far = opposite(lax.dynamic_slice_in_dim(near, lax.axis_index("c") * half, half, 0))
    return (near, shift(near, "c", 1), far, shift(far, "c", 1))


def vmem():
    return pl.BlockSpec(memory_space=pltpu.VMEM)


def smem():
    return pl.BlockSpec(memory_space=pltpu.SMEM)


def cost(flops, moved, exps=0):
    return pl.CostEstimate(flops=flops, bytes_accessed=moved, transcendentals=exps)


def light_kernel(first_ref, q_ref, prev_ref, own_ref, next_ref, out_ref, padded, *, total):
    rows, width = q_ref.shape
    tile = 2 * HALO
    span = tile + 2 * HALO
    padded[:HALO] = prev_ref[...]
    padded[HALO : HALO + rows] = own_ref[...]
    padded[HALO + rows :] = next_ref[...]
    row = lax.broadcasted_iota(jnp.int32, (tile, span), 0)
    col = lax.broadcasted_iota(jnp.int32, (tile, span), 1)
    near = jnp.abs(col - HALO - row) <= RADIUS
    head_of = lax.broadcasted_iota(jnp.int32, (tile, width), 1) // HDIM

    def tile_step(number, unused):
        start = pl.multiple_of(number * tile, tile)
        position = first_ref[0] + start - HALO + col
        allowed = near & (position >= 0) & (position < total)
        q = q_ref[pl.ds(start, tile), :].astype(jnp.float32) * (HDIM**-0.5)
        keys = padded[pl.ds(start, span), :width]
        values = padded[pl.ds(start, span), width:]
        out = jnp.zeros((tile, width), jnp.float32)
        for head in range(width // HDIM):
            scores = lax.dot_general(
                jnp.where(head_of == head, q, 0.0).astype(jnp.bfloat16),
                keys,
                (((1,), (1,)), ((), ())),
                preferred_element_type=jnp.float32,
            )
            scores = jnp.where(allowed, scores, LOW)
            weights = jnp.exp(scores - jnp.max(scores, axis=1, keepdims=True))
            totals = jnp.sum(weights, axis=1, keepdims=True)
            mixed = jnp.dot(
                weights.astype(jnp.bfloat16), values, preferred_element_type=jnp.float32
            )
            out = jnp.where(head_of == head, mixed / totals, out)
        out_ref[pl.ds(start, tile), :] = out.astype(jnp.bfloat16)
        return unused

    lax.fori_loop(0, rows // tile, tile_step, 0)


def slot_list(index_ref, bound, cap):
    lines, lanes = index_ref.shape
    begin = jnp.sum(jnp.where(index_ref[...] < bound, 1.0, 0.0)).astype(jnp.int32)
    line = begin // lanes
    count = (cap + lanes - 1) // lanes + 1
    parts = []
    for step in range(count):
        values = index_ref[pl.ds(jnp.minimum(line + step, lines - 1), 1), :]
        parts.append(jnp.where(line + step < lines, values, -1))
    window = jnp.broadcast_to(jnp.concatenate(parts, axis=1), (8, count * lanes))
    size = count * lanes
    return pltpu.roll(window, (size - begin % lanes) % size, 1)[:1, :cap]


def hot_of(slots, rows):
    token = lax.broadcasted_iota(jnp.int32, (rows, slots.shape[1]), 0)
    return jnp.where(token == slots, 1.0, 0.0).astype(jnp.bfloat16)


def pick_rows(hot, rows):
    return lax.dot_general(
        hot, rows, (((0,), (0,)), ((), ())), preferred_element_type=jnp.float32
    ).astype(jnp.bfloat16)


def pick_kernel(place_ref, index_ref, tokens_ref, *refs):
    outs, picked = refs[:-1], refs[-1]
    groups = len(outs)
    quarter = outs[0].shape[0]
    rows = tokens_ref.shape[0]
    slots = slot_list(index_ref, place_ref[4], groups * quarter) - place_ref[5]
    picked[...] = pick_rows(hot_of(slots, rows), tokens_ref[...])
    for step in range(groups):
        group = (place_ref[3] + step) % groups
        outs[step][...] = picked[pl.ds(pl.multiple_of(group * quarter, 16), quarter), :]


def local_kernel(
    tokens_ref, query_ref, key_ref, value_ref, q_ref, pair_ref, head_ref, tail_ref
):
    rows = tokens_ref.shape[0]
    width = query_ref.shape[1]
    tile = rows // 2

    def tile_step(number, unused):
        span = pl.ds(pl.multiple_of(number * tile, tile), tile)
        tokens = tokens_ref[span, :]

        def times(weights):
            return jnp.dot(tokens, weights[...], preferred_element_type=jnp.float32).astype(
                jnp.bfloat16
            )

        q_ref[span, :] = times(query_ref)
        pair_ref[span, :width] = times(key_ref)
        pair_ref[span, width:] = times(value_ref)
        return unused

    lax.fori_loop(0, 2, tile_step, 0)
    head_ref[...] = pair_ref[:HALO]
    tail_ref[...] = pair_ref[rows - HALO :]


def project_kernel(
    place_ref, index_ref, tokens_ref, own_ref, near_ref, near2_ref, far_ref, far2_ref, *refs
):
    outs, slots_ref, far, dense = refs[:-3], refs[-3], refs[-2], refs[-1]
    core = place_ref[2]
    half = far_ref.shape[0]
    rows = tokens_ref.shape[0]
    tile = rows // 2
    far[pl.ds(pl.multiple_of(core * half, half), half), :] = far_ref[...]
    far[pl.ds(pl.multiple_of((1 - core) * half, half), half), :] = far2_ref[...]

    def tile_step(number, unused):
        span = pl.ds(pl.multiple_of(number * tile, tile), tile)
        tokens = tokens_ref[span, :]
        for group, weights in ((0, own_ref), (1 + core, near_ref), (2 - core, near2_ref), (3, far)):
            dense[group, span, :] = jnp.dot(
                tokens, weights[...], preferred_element_type=jnp.float32
            ).astype(jnp.bfloat16)
        return unused

    lax.fori_loop(0, 2, tile_step, 0)
    slots = slot_list(index_ref, place_ref[4], slots_ref.shape[1]) - place_ref[5]
    slots_ref[...] = slots
    hot = hot_of(slots, rows)
    for group, out in enumerate(outs):
        out[...] = pick_rows(hot, dense[group])


def pair_kernel(place_ref, own_ref, a_ref, b_ref, c_ref, key_ref, value_ref, out_ref, rows):
    quarter = own_ref.shape[0]
    for number, source in enumerate((own_ref, a_ref, b_ref, c_ref)):
        group = (place_ref[3] - number + 4) % 4
        rows[pl.ds(pl.multiple_of(group * quarter, 16), quarter), :] = source[...]
    every = rows[...]
    keys = jnp.dot(every, key_ref[...], preferred_element_type=jnp.float32).astype(jnp.bfloat16)
    values = jnp.dot(every, value_ref[...], preferred_element_type=jnp.float32).astype(
        jnp.bfloat16
    )
    size = 4 * quarter
    for head in range(out_ref.shape[0] // size):
        cols = slice(head * HDIM, (head + 1) * HDIM)
        out_ref[head * size : (head + 1) * size, :] = jnp.concatenate(
            [keys[:, cols], values[:, cols]], axis=1
        )


def query_kernel(own_ref, a_ref, b_ref, c_ref, out_ref):
    rows = own_ref[...] + a_ref[...] + b_ref[...] + c_ref[...]
    half = rows.shape[0] // 2
    for head in range(out_ref.shape[0] // half):
        cols = slice(head * HDIM, (head + 1) * HDIM)
        out_ref[head * half : (head + 1) * half, :] = jnp.concatenate(
            [rows[:half, cols], rows[half:, cols]], axis=1
        )


def exchange(value):
    return lax.all_to_all(value, "y", 0, 0, tiled=True)


def attention_kernel(place_ref, query_starts_ref, key_starts_ref, *refs, sizes):
    y_size, z_size = sizes
    q_ref, refs = refs[0], refs[1:]
    near_refs, refs = refs[:z_size], refs[z_size:]
    far_refs, refs = refs[:z_size], refs[z_size:]
    out_ref, queries, keys, values, results = refs
    pz, pc = place_ref[1], place_ref[2]
    half = q_ref.shape[0] // y_size
    key_cap = near_refs[0].shape[0] // y_size

    def block_of(by, step_z, swap):
        bz = (pz + step_z + z_size) % z_size
        bc = (pc + swap) % 2
        return (by * z_size + bz) * 2 + bc

    lane = lax.broadcasted_iota(jnp.int32, (key_cap, 2 * HDIM), 1)
    slot_ids = lax.broadcasted_iota(jnp.int32, (key_cap, 1), 0)
    total = 0
    for swap, sources in ((0, near_refs), (1, far_refs)):
        for step_z, source in zip(Z_STEPS, sources):

            def place_piece(by, total, swap=swap, step_z=step_z, source=source):
                block = block_of(by, step_z, swap)
                count = key_starts_ref[block + 1] - key_starts_ref[block]
                start = pl.multiple_of(by * key_cap, 16)
                pair = source[pl.ds(start, key_cap), :].astype(jnp.float32)
                valid = slot_ids < count
                target = pl.ds(pl.multiple_of(total, 16), key_cap)
                keys[target, :] = jnp.where(
                    lane < HDIM,
                    pair,
                    jnp.where(lane == HDIM, jnp.where(valid, 0.0, LOW), 0.0),
                ).astype(jnp.bfloat16)
                values[target, :] = jnp.where(
                    lane >= HDIM,
                    pair,
                    jnp.where(lane == 0, jnp.where(valid, 1.0, 0.0), 0.0),
                ).astype(jnp.bfloat16)
                return total + (count + 15) // 16 * 16

            total = lax.fori_loop(0, y_size, place_piece, total)
    tail_lane = lax.broadcasted_iota(jnp.int32, (KCHUNK, 2 * HDIM), 1)
    tail = pl.ds(pl.multiple_of(total, 16), KCHUNK)
    keys[tail, :] = jnp.where(tail_lane == HDIM, LOW, 0.0).astype(jnp.bfloat16)
    values[tail, :] = jnp.zeros((KCHUNK, 2 * HDIM), jnp.bfloat16)

    queries[...] = jnp.zeros_like(queries)
    results[...] = jnp.zeros_like(results)
    q_lane = lax.broadcasted_iota(jnp.int32, (half, 2 * HDIM), 1)
    offsets = []
    offset = 0
    for by in range(y_size):
        block = block_of(by, 0, 0)
        count = query_starts_ref[block + 1] - query_starts_ref[block]
        offsets.append(offset)
        packed = q_ref[by * half : (by + 1) * half, :].astype(jnp.float32) * (HDIM**-0.5)
        rolled = pltpu.roll(packed, HDIM, 1)
        for number, value in ((0, packed), (1, rolled)):
            filled = jnp.where(q_lane < HDIM, value, jnp.where(q_lane == HDIM, 1.0, 0.0))
            queries[pl.ds(pl.multiple_of(offset + number * half, 16), half), :] = filled.astype(
                jnp.bfloat16
            )
        offset = offset + (count + 15) // 16 * 16
    chunks = (total + KCHUNK - 1) // KCHUNK

    def tile_step(tile, unused):
        rows = pl.ds(pl.multiple_of(tile * QTILE, QTILE), QTILE)
        q = queries[rows, :]

        def chunk_step(chunk, state):
            peak, acc = state
            span = pl.ds(pl.multiple_of(chunk * KCHUNK, KCHUNK), KCHUNK)
            scores = lax.dot_general(
                q, keys[span, :], (((1,), (1,)), ((), ())), preferred_element_type=jnp.float32
            )
            new_peak = jnp.maximum(peak, jnp.max(scores, axis=1, keepdims=True))
            weights = jnp.exp(scores - new_peak).astype(jnp.bfloat16)
            acc = acc * jnp.exp(peak - new_peak) + jnp.dot(
                weights, values[span, :], preferred_element_type=jnp.float32
            )
            return new_peak, acc

        _, acc = lax.fori_loop(
            0,
            chunks,
            chunk_step,
            (
                jnp.full((QTILE, 1), LOW, jnp.float32),
                jnp.zeros((QTILE, 2 * HDIM), jnp.float32),
            ),
        )
        results[rows, :] = (acc / acc[:, 0:1]).astype(jnp.bfloat16)
        return unused

    lax.fori_loop(0, (offset + QTILE - 1) // QTILE, tile_step, 0)

    for by in range(y_size):
        first = results[pl.ds(pl.multiple_of(offsets[by], 16), half), :]
        second = results[pl.ds(pl.multiple_of(offsets[by] + half, 16), half), :]
        out_ref[by * half : (by + 1) * half, :] = jnp.concatenate(
            [first[:, HDIM:], second[:, HDIM:]], axis=1
        )


def final_kernel(
    place_ref,
    slots_ref,
    light_ref,
    light_out_ref,
    m0_ref,
    m1_ref,
    m2_ref,
    m3_ref,
    own_ref,
    near_ref,
    near2_ref,
    far_ref,
    far2_ref,
    out_ref,
    mixed,
):
    pc = place_ref[2]
    rows = light_ref.shape[0]
    heads = 4
    half = m0_ref.shape[0] // heads

    @pl.when(pl.program_id(0) == 0)
    def _():
        slots = slots_ref.shape[1]
        token = lax.broadcasted_iota(jnp.int32, (rows, slots), 0)
        place = jnp.where(token == slots_ref[...], 1.0, 0.0).astype(jnp.bfloat16)
        for number, source in enumerate((m0_ref, m1_ref, m2_ref, m3_ref)):
            parts = []
            for position in range(heads):
                head = (position + 2 * pc) % heads if number == 3 else position
                packed = source[pl.ds(pl.multiple_of(head * half, half), half), :]
                parts.append(jnp.concatenate([packed[:, :HDIM], packed[:, HDIM:]], axis=0))
            wide = jnp.concatenate(parts, axis=1)
            mixed[number] = jnp.dot(place, wide, preferred_element_type=jnp.float32).astype(
                jnp.bfloat16
            )

    acc = jnp.dot(light_ref[...], light_out_ref[...], preferred_element_type=jnp.float32)
    acc += jnp.dot(mixed[0], own_ref[...], preferred_element_type=jnp.float32)
    acc += jnp.dot(mixed[1 + pc], near_ref[...], preferred_element_type=jnp.float32)
    acc += jnp.dot(mixed[2 - pc], near2_ref[...], preferred_element_type=jnp.float32)
    far = jnp.concatenate([far_ref[...], far2_ref[...]], axis=0)
    acc += jnp.dot(mixed[3], far, preferred_element_type=jnp.float32)
    out_ref[...] = acc.astype(out_ref.dtype)


def layer(
    tokens,
    query_index,
    key_index,
    light_query,
    light_key,
    light_value,
    light_out,
    heavy_query,
    heavy_key,
    heavy_value,
    heavy_out,
):
    rows, model = tokens.shape
    y_size, z_size, x_size = lax.axis_size("y"), lax.axis_size("z"), lax.axis_size("x")
    blocks = y_size * z_size * 2
    block_len = rows * x_size
    py, pz, pc, px = (lax.axis_index(a) for a in ALL_AXES)
    block = (py * z_size + pz) * 2 + pc
    first = (block * x_size + px) * rows
    query_cap = block_len // 4
    key_cap = 3 * block_len // 32
    quarter = key_cap // x_size
    width = light_query.shape[1]
    heavy_width = heavy_query.shape[1]
    bf16 = jnp.bfloat16
    place = jnp.stack([py, pz, pc, px, block * block_len, first]).astype(jnp.int32)
    key_lines = key_index.reshape(-1, 128)
    query_lines = query_index.reshape(-1, 128)

    def array(*shape):
        return jax.ShapeDtypeStruct(shape, bf16)

    wq = gather_weights(heavy_query)

    picked = pl.pallas_call(
        pick_kernel,
        out_shape=[array(quarter, model)] * x_size,
        in_specs=[smem()] + [vmem()] * 2,
        out_specs=[vmem()] * x_size,
        scratch_shapes=[pltpu.VMEM((key_cap, model), bf16)],
        cost_estimate=cost(2 * key_cap * rows * model, 2 * rows * model),
        name="pick",
    )(place, key_lines, tokens)
    arrived = [shift(picked[step], "x", step) for step in (1, 3, 2)]
    piece = picked[0] + arrived[0] + arrived[1] + arrived[2]
    row_pieces = [piece] + [shift(piece, "x", step) for step in (1, 2, 3)]

    light_rows, light_pair, head, tail = pl.pallas_call(
        local_kernel,
        out_shape=[array(rows, width), array(rows, 2 * width)] + [array(HALO, 2 * width)] * 2,
        in_specs=[vmem()] * 4,
        out_specs=[vmem()] * 4,
        cost_estimate=cost(6 * rows * width * model, 2 * rows * model + 6 * model * width),
        name="light_project",
    )(tokens, light_query, light_key, light_value)
    devices = blocks * x_size
    up = [(i, i + 1) for i in range(devices - 1)]
    before = lax.ppermute(tail, ALL_AXES, up)
    after = lax.ppermute(head, ALL_AXES, [(b, a) for a, b in up])
    light_mixed = pl.pallas_call(
        functools.partial(light_kernel, total=rows * devices),
        out_shape=array(rows, width),
        in_specs=[smem()] + [vmem()] * 4,
        out_specs=vmem(),
        scratch_shapes=[pltpu.VMEM((rows + 2 * HALO, 2 * width), bf16)],
        cost_estimate=cost(4 * rows * 512 * 256 * 4, 4 * rows * width * 2, 4 * rows * 512),
        name="light",
    )(first.reshape(1), light_rows, before, light_pair, after)

    bounds = jnp.arange(blocks + 1, dtype=jnp.int32) * block_len
    key_starts = jnp.sum((key_index[None, :] < bounds[:, None]).astype(jnp.int32), axis=1)
    query_starts = jnp.sum((query_index[None, :] < bounds[:, None]).astype(jnp.int32), axis=1)

    pairs = pl.pallas_call(
        pair_kernel,
        out_shape=array(y_size * key_cap, 2 * HDIM),
        in_specs=[smem()] + [vmem()] * 6,
        out_specs=vmem(),
        scratch_shapes=[pltpu.VMEM((key_cap, model), bf16)],
        cost_estimate=cost(4 * key_cap * model * heavy_width, 4 * model * heavy_width),
        name="key_value_heads",
    )(place, *row_pieces, heavy_key, heavy_value)
    column = exchange(pairs)

    *projected, query_slots = pl.pallas_call(
        project_kernel,
        out_shape=[array(query_cap, heavy_width)] * x_size
        + [jax.ShapeDtypeStruct((1, query_cap), jnp.int32)],
        in_specs=[smem()] + [vmem()] * 7,
        out_specs=[vmem()] * (x_size + 1),
        scratch_shapes=[
            pltpu.VMEM((model, heavy_width), bf16),
            pltpu.VMEM((x_size, rows, heavy_width), bf16),
        ],
        cost_estimate=cost(8 * query_cap * model * heavy_width, 8 * model * heavy_width),
        name="query_project",
    )(place, query_lines, tokens, heavy_query, *wq)
    q_in = [shift(projected[i + 1], "x", step) for i, step in enumerate((-1, 1, 2))]
    q_heads = pl.pallas_call(
        query_kernel,
        out_shape=array(y_size * query_cap // 2, 2 * HDIM),
        in_specs=[vmem()] * 4,
        out_specs=vmem(),
        cost_estimate=cost(4 * query_cap * heavy_width, 10 * query_cap * heavy_width),
        name="query_heads",
    )(projected[0], *q_in)
    q_column = exchange(q_heads)

    wo = gather_weights(heavy_out)

    ring = {0: column}
    for step in range(1, z_size // 2 + 1):
        ring[-step] = shift(ring[-step + 1], "z", 1)
        if step < z_size // 2:
            ring[step] = shift(ring[step - 1], "z", -1)
    near_pairs = [ring[s] for s in Z_STEPS]
    far_pairs = [shift(ring[s], "c", 1) for s in Z_STEPS]

    key_total = 2 * z_size * column.shape[0]
    slots_total = y_size * query_cap + QTILE
    heads_out = pl.pallas_call(
        functools.partial(attention_kernel, sizes=(y_size, z_size)),
        out_shape=array(y_size * query_cap // 2, 2 * HDIM),
        in_specs=[smem()] * 3 + [vmem()] * (1 + 2 * z_size),
        out_specs=vmem(),
        scratch_shapes=[
            pltpu.VMEM((slots_total, 2 * HDIM), bf16),
            pltpu.VMEM((key_total + KCHUNK, 2 * HDIM), bf16),
            pltpu.VMEM((key_total + KCHUNK, 2 * HDIM), bf16),
            pltpu.VMEM((slots_total, 2 * HDIM), bf16),
        ],
        cost_estimate=cost(4 * 1024 * key_total * 256, 4 * key_total * HDIM, 1024 * key_total),
        name="heavy_attention",
    )(place, query_starts, key_starts, q_column, *near_pairs, *far_pairs)

    back = exchange(heads_out)
    groups = [back] + [shift(back, "x", step) for step in (1, -1, 2)]
    tile = 512

    def whole(*shape):
        return pl.BlockSpec(shape, lambda j: (0,) * len(shape))

    def columns(count):
        return pl.BlockSpec((count, tile), lambda j: (0, j))

    return pl.pallas_call(
        final_kernel,
        grid=(model // tile,),
        out_shape=array(rows, model),
        in_specs=[smem(), whole(1, query_cap), whole(rows, width), columns(width)]
        + [whole(y_size * query_cap // 2, 2 * HDIM)] * 4
        + [columns(heavy_width)]
        + [columns(p.shape[0]) for p in wo],
        out_specs=columns(rows),
        scratch_shapes=[pltpu.VMEM((4, rows, heavy_width), bf16)],
        cost_estimate=cost(2 * rows * 1280 * model, 10 * rows * model),
        name="combine",
    )(
        place,
        query_slots,
        light_mixed,
        light_out,
        *groups,
        heavy_out,
        *wo,
    )


def solution(mesh):
    torus = Mesh(mesh.devices.reshape(4, 8, 2, mesh.shape["head"]), ALL_AXES)
    return jax.shard_map(
        layer,
        mesh=torus,
        in_specs=(P(ALL_AXES, None),)
        + (P(),) * 6
        + (P(None, "x"),) * 3
        + (P("x", None),),
        out_specs=P(ALL_AXES, None),
        check_vma=False,
    )
```

```python
import functools

import jax
import jax.numpy as jnp
from jax import lax
from jax.experimental import pallas as pl
from jax.experimental.pallas import tpu as pltpu
from jax.sharding import Mesh
from jax.sharding import PartitionSpec as P


HDIM = 64
RADIUS = 127
HALO = 128
ALL_AXES = ("y", "z", "c", "x")
LOW = -1e30
QTILE = 512
KCHUNK = 3072
Z_STEPS = (0, -1, 1, -2, 2, -3, 3, -4)


def shift(value, axis, distance):
    size = lax.axis_size(axis)
    return lax.ppermute(value, axis, [(i, (i + distance) % size) for i in range(size)])


def opposite(value):
    size = lax.axis_size("x")
    pairs = [(i, (i + 1) % size) for i in range(size)]
    pairs += [(size + i, size + (i - 1) % size) for i in range(size)]
    return lax.ppermute(value, ("c", "x"), pairs)


def gather_weights(shard):
    near = opposite(shard)
    half = shard.shape[0] // 2
    far = opposite(lax.dynamic_slice_in_dim(near, lax.axis_index("c") * half, half, 0))
    return (near, shift(near, "c", 1), far, shift(far, "c", 1))


def vmem():
    return pl.BlockSpec(memory_space=pltpu.VMEM)


def smem():
    return pl.BlockSpec(memory_space=pltpu.SMEM)


def cost(flops, moved, exps=0):
    return pl.CostEstimate(flops=flops, bytes_accessed=moved, transcendentals=exps)


def light_kernel(first_ref, q_ref, prev_ref, own_ref, next_ref, out_ref, padded, *, total):
    rows, width = q_ref.shape
    tile = 2 * HALO
    span = tile + 2 * HALO
    padded[:HALO] = prev_ref[...]
    padded[HALO : HALO + rows] = own_ref[...]
    padded[HALO + rows :] = next_ref[...]
    row = lax.broadcasted_iota(jnp.int32, (tile, span), 0)
    col = lax.broadcasted_iota(jnp.int32, (tile, span), 1)
    near = jnp.abs(col - HALO - row) <= RADIUS
    head_of = lax.broadcasted_iota(jnp.int32, (tile, width), 1) // HDIM

    def tile_step(number, unused):
        start = pl.multiple_of(number * tile, tile)
        position = first_ref[0] + start - HALO + col
        allowed = near & (position >= 0) & (position < total)
        q = q_ref[pl.ds(start, tile), :].astype(jnp.float32) * (HDIM**-0.5)
        keys = padded[pl.ds(start, span), :width]
        values = padded[pl.ds(start, span), width:]
        out = jnp.zeros((tile, width), jnp.float32)
        for head in range(width // HDIM):
            scores = lax.dot_general(
                jnp.where(head_of == head, q, 0.0).astype(jnp.bfloat16),
                keys,
                (((1,), (1,)), ((), ())),
                preferred_element_type=jnp.float32,
            )
            scores = jnp.where(allowed, scores, LOW)
            weights = jnp.exp(scores - jnp.max(scores, axis=1, keepdims=True))
            totals = jnp.sum(weights, axis=1, keepdims=True)
            mixed = jnp.dot(
                weights.astype(jnp.bfloat16), values, preferred_element_type=jnp.float32
            )
            out = jnp.where(head_of == head, mixed / totals, out)
        out_ref[pl.ds(start, tile), :] = out.astype(jnp.bfloat16)
        return unused

    lax.fori_loop(0, rows // tile, tile_step, 0)


def slot_list(index_ref, bound, cap):
    lines, lanes = index_ref.shape
    begin = jnp.sum(jnp.where(index_ref[...] < bound, 1.0, 0.0)).astype(jnp.int32)
    line = begin // lanes
    count = (cap + lanes - 1) // lanes + 1
    parts = []
    for step in range(count):
        values = index_ref[pl.ds(jnp.minimum(line + step, lines - 1), 1), :]
        parts.append(jnp.where(line + step < lines, values, -1))
    window = jnp.broadcast_to(jnp.concatenate(parts, axis=1), (8, count * lanes))
    size = count * lanes
    return pltpu.roll(window, (size - begin % lanes) % size, 1)[:1, :cap]


def hot_of(slots, rows):
    token = lax.broadcasted_iota(jnp.int32, (rows, slots.shape[1]), 0)
    return jnp.where(token == slots, 1.0, 0.0).astype(jnp.bfloat16)


def pick_rows(hot, rows):
    return lax.dot_general(
        hot, rows, (((0,), (0,)), ((), ())), preferred_element_type=jnp.float32
    ).astype(jnp.bfloat16)


def pick_kernel(place_ref, index_ref, tokens_ref, *refs):
    outs, picked = refs[:-1], refs[-1]
    groups = len(outs)
    quarter = outs[0].shape[0]
    rows = tokens_ref.shape[0]
    slots = slot_list(index_ref, place_ref[4], groups * quarter) - place_ref[5]
    picked[...] = pick_rows(hot_of(slots, rows), tokens_ref[...])
    for step in range(groups):
        group = (place_ref[3] + step) % groups
        outs[step][...] = picked[pl.ds(pl.multiple_of(group * quarter, 16), quarter), :]


def local_kernel(
    tokens_ref, query_ref, key_ref, value_ref, q_ref, pair_ref, head_ref, tail_ref
):
    rows = tokens_ref.shape[0]
    width = query_ref.shape[1]
    tile = rows // 2

    def tile_step(number, unused):
        span = pl.ds(pl.multiple_of(number * tile, tile), tile)
        tokens = tokens_ref[span, :]

        def times(weights):
            return jnp.dot(tokens, weights[...], preferred_element_type=jnp.float32).astype(
                jnp.bfloat16
            )

        q_ref[span, :] = times(query_ref)
        pair_ref[span, :width] = times(key_ref)
        pair_ref[span, width:] = times(value_ref)
        return unused

    lax.fori_loop(0, 2, tile_step, 0)
    head_ref[...] = pair_ref[:HALO]
    tail_ref[...] = pair_ref[rows - HALO :]


def project_kernel(
    place_ref, index_ref, tokens_ref, own_ref, near_ref, near2_ref, far_ref, far2_ref, *refs
):
    outs, slots_ref, far, dense = refs[:-3], refs[-3], refs[-2], refs[-1]
    core = place_ref[2]
    half = far_ref.shape[0]
    rows = tokens_ref.shape[0]
    tile = rows // 2
    far[pl.ds(pl.multiple_of(core * half, half), half), :] = far_ref[...]
    far[pl.ds(pl.multiple_of((1 - core) * half, half), half), :] = far2_ref[...]

    def tile_step(number, unused):
        span = pl.ds(pl.multiple_of(number * tile, tile), tile)
        tokens = tokens_ref[span, :]
        for group, weights in ((0, own_ref), (1 + core, near_ref), (2 - core, near2_ref), (3, far)):
            dense[group, span, :] = jnp.dot(
                tokens, weights[...], preferred_element_type=jnp.float32
            ).astype(jnp.bfloat16)
        return unused

    lax.fori_loop(0, 2, tile_step, 0)
    slots = slot_list(index_ref, place_ref[4], slots_ref.shape[1]) - place_ref[5]
    slots_ref[...] = slots
    hot = hot_of(slots, rows)
    for group, out in enumerate(outs):
        out[...] = pick_rows(hot, dense[group])


def pair_kernel(place_ref, own_ref, a_ref, b_ref, c_ref, key_ref, value_ref, out_ref, rows):
    quarter = own_ref.shape[0]
    for number, source in enumerate((own_ref, a_ref, b_ref, c_ref)):
        group = (place_ref[3] - number + 4) % 4
        rows[pl.ds(pl.multiple_of(group * quarter, 16), quarter), :] = source[...]
    every = rows[...]
    keys = jnp.dot(every, key_ref[...], preferred_element_type=jnp.float32).astype(jnp.bfloat16)
    values = jnp.dot(every, value_ref[...], preferred_element_type=jnp.float32).astype(
        jnp.bfloat16
    )
    size = 4 * quarter
    for head in range(out_ref.shape[0] // size):
        cols = slice(head * HDIM, (head + 1) * HDIM)
        out_ref[head * size : (head + 1) * size, :] = jnp.concatenate(
            [keys[:, cols], values[:, cols]], axis=1
        )


def query_kernel(own_ref, a_ref, b_ref, c_ref, out_ref):
    rows = own_ref[...] + a_ref[...] + b_ref[...] + c_ref[...]
    half = rows.shape[0] // 2
    for head in range(out_ref.shape[0] // half):
        cols = slice(head * HDIM, (head + 1) * HDIM)
        out_ref[head * half : (head + 1) * half, :] = jnp.concatenate(
            [rows[:half, cols], rows[half:, cols]], axis=1
        )


def exchange(value):
    return lax.all_to_all(value, "y", 0, 0, tiled=True)


def attention_kernel(place_ref, query_starts_ref, key_starts_ref, *refs, sizes):
    y_size, z_size = sizes
    q_ref, refs = refs[0], refs[1:]
    near_refs, refs = refs[:z_size], refs[z_size:]
    far_refs, refs = refs[:z_size], refs[z_size:]
    out_ref, queries, keys, values, results = refs
    pz, pc = place_ref[1], place_ref[2]
    half = q_ref.shape[0] // y_size
    key_cap = near_refs[0].shape[0] // y_size

    def block_of(by, step_z, swap):
        bz = (pz + step_z + z_size) % z_size
        bc = (pc + swap) % 2
        return (by * z_size + bz) * 2 + bc

    lane = lax.broadcasted_iota(jnp.int32, (key_cap, 2 * HDIM), 1)
    slot_ids = lax.broadcasted_iota(jnp.int32, (key_cap, 1), 0)
    total = 0
    for swap, sources in ((0, near_refs), (1, far_refs)):
        for step_z, source in zip(Z_STEPS, sources):

            def place_piece(by, total, swap=swap, step_z=step_z, source=source):
                block = block_of(by, step_z, swap)
                count = key_starts_ref[block + 1] - key_starts_ref[block]
                start = pl.multiple_of(by * key_cap, 16)
                pair = source[pl.ds(start, key_cap), :].astype(jnp.float32)
                valid = slot_ids < count
                target = pl.ds(pl.multiple_of(total, 16), key_cap)
                keys[target, :] = jnp.where(
                    lane < HDIM,
                    pair,
                    jnp.where(lane == HDIM, jnp.where(valid, 0.0, LOW), 0.0),
                ).astype(jnp.bfloat16)
                values[target, :] = jnp.where(
                    lane >= HDIM,
                    pair,
                    jnp.where(lane == 0, jnp.where(valid, 1.0, 0.0), 0.0),
                ).astype(jnp.bfloat16)
                return total + (count + 15) // 16 * 16

            total = lax.fori_loop(0, y_size, place_piece, total)
    tail_lane = lax.broadcasted_iota(jnp.int32, (KCHUNK, 2 * HDIM), 1)
    tail = pl.ds(pl.multiple_of(total, 16), KCHUNK)
    keys[tail, :] = jnp.where(tail_lane == HDIM, LOW, 0.0).astype(jnp.bfloat16)
    values[tail, :] = jnp.zeros((KCHUNK, 2 * HDIM), jnp.bfloat16)

    queries[...] = jnp.zeros_like(queries)
    results[...] = jnp.zeros_like(results)
    q_lane = lax.broadcasted_iota(jnp.int32, (half, 2 * HDIM), 1)
    offsets = []
    offset = 0
    for by in range(y_size):
        block = block_of(by, 0, 0)
        count = query_starts_ref[block + 1] - query_starts_ref[block]
        offsets.append(offset)
        packed = q_ref[by * half : (by + 1) * half, :].astype(jnp.float32) * (HDIM**-0.5)
        rolled = pltpu.roll(packed, HDIM, 1)
        for number, value in ((0, packed), (1, rolled)):
            filled = jnp.where(q_lane < HDIM, value, jnp.where(q_lane == HDIM, 1.0, 0.0))
            queries[pl.ds(pl.multiple_of(offset + number * half, 16), half), :] = filled.astype(
                jnp.bfloat16
            )
        offset = offset + (count + 15) // 16 * 16
    chunks = (total + KCHUNK - 1) // KCHUNK

    def tile_step(tile, unused):
        rows = pl.ds(pl.multiple_of(tile * QTILE, QTILE), QTILE)
        q = queries[rows, :]

        def chunk_step(chunk, state):
            peak, acc = state
            span = pl.ds(pl.multiple_of(chunk * KCHUNK, KCHUNK), KCHUNK)
            scores = lax.dot_general(
                q, keys[span, :], (((1,), (1,)), ((), ())), preferred_element_type=jnp.float32
            )
            new_peak = jnp.maximum(peak, jnp.max(scores, axis=1, keepdims=True))
            weights = jnp.exp(scores - new_peak).astype(jnp.bfloat16)
            acc = acc * jnp.exp(peak - new_peak) + jnp.dot(
                weights, values[span, :], preferred_element_type=jnp.float32
            )
            return new_peak, acc

        _, acc = lax.fori_loop(
            0,
            chunks,
            chunk_step,
            (
                jnp.full((QTILE, 1), LOW, jnp.float32),
                jnp.zeros((QTILE, 2 * HDIM), jnp.float32),
            ),
        )
        results[rows, :] = (acc / acc[:, 0:1]).astype(jnp.bfloat16)
        return unused

    lax.fori_loop(0, (offset + QTILE - 1) // QTILE, tile_step, 0)

    for by in range(y_size):
        first = results[pl.ds(pl.multiple_of(offsets[by], 16), half), :]
        second = results[pl.ds(pl.multiple_of(offsets[by] + half, 16), half), :]
        out_ref[by * half : (by + 1) * half, :] = jnp.concatenate(
            [first[:, HDIM:], second[:, HDIM:]], axis=1
        )


def placed(slots_ref, source, rows, turn):
    heads = 4
    half = source.shape[0] // heads
    parts = []
    for position in range(heads):
        head = (position + 2 * turn) % heads
        start = head * half
        packed = source[pl.ds(start if isinstance(turn, int) else pl.multiple_of(start, half), half), :]
        parts.append(jnp.concatenate([packed[:, :HDIM], packed[:, HDIM:]], axis=0))
    hot = hot_of(slots_ref[...], rows)
    wide = jnp.concatenate(parts, axis=1)
    return jnp.dot(hot, wide, preferred_element_type=jnp.float32).astype(jnp.bfloat16)


def own_kernel(slots_ref, light_ref, light_out_ref, source_ref, own_ref, out_ref, mixed):
    @pl.when(pl.program_id(0) == 0)
    def _():
        mixed[...] = placed(slots_ref, source_ref, light_ref.shape[0], 0)

    acc = jnp.dot(light_ref[...], light_out_ref[...], preferred_element_type=jnp.float32)
    out_ref[...] = acc + jnp.dot(mixed[...], own_ref[...], preferred_element_type=jnp.float32)


def final_kernel(
    place_ref,
    slots_ref,
    sum_ref,
    m1_ref,
    m2_ref,
    m3_ref,
    near_ref,
    near2_ref,
    far_ref,
    far2_ref,
    out_ref,
    mixed,
):
    pc = place_ref[2]

    @pl.when(pl.program_id(0) == 0)
    def _():
        for number, source in enumerate((m1_ref, m2_ref, m3_ref)):
            mixed[number] = placed(slots_ref, source, sum_ref.shape[0], pc if number == 2 else 0)

    acc = sum_ref[...]
    acc += jnp.dot(mixed[pc], near_ref[...], preferred_element_type=jnp.float32)
    acc += jnp.dot(mixed[1 - pc], near2_ref[...], preferred_element_type=jnp.float32)
    far = jnp.concatenate([far_ref[...], far2_ref[...]], axis=0)
    acc += jnp.dot(mixed[2], far, preferred_element_type=jnp.float32)
    out_ref[...] = acc.astype(out_ref.dtype)


def layer(
    tokens,
    query_index,
    key_index,
    light_query,
    light_key,
    light_value,
    light_out,
    heavy_query,
    heavy_key,
    heavy_value,
    heavy_out,
):
    rows, model = tokens.shape
    y_size, z_size, x_size = lax.axis_size("y"), lax.axis_size("z"), lax.axis_size("x")
    blocks = y_size * z_size * 2
    block_len = rows * x_size
    py, pz, pc, px = (lax.axis_index(a) for a in ALL_AXES)
    block = (py * z_size + pz) * 2 + pc
    first = (block * x_size + px) * rows
    query_cap = block_len // 4
    key_cap = 3 * block_len // 32
    quarter = key_cap // x_size
    width = light_query.shape[1]
    heavy_width = heavy_query.shape[1]
    bf16 = jnp.bfloat16
    place = jnp.stack([py, pz, pc, px, block * block_len, first]).astype(jnp.int32)
    key_lines = key_index.reshape(-1, 128)
    query_lines = query_index.reshape(-1, 128)

    def array(*shape):
        return jax.ShapeDtypeStruct(shape, bf16)

    wq = gather_weights(heavy_query)

    picked = pl.pallas_call(
        pick_kernel,
        out_shape=[array(quarter, model)] * x_size,
        in_specs=[smem()] + [vmem()] * 2,
        out_specs=[vmem()] * x_size,
        scratch_shapes=[pltpu.VMEM((key_cap, model), bf16)],
        cost_estimate=cost(2 * key_cap * rows * model, 2 * rows * model),
        name="pick",
    )(place, key_lines, tokens)
    arrived = [shift(picked[step], "x", step) for step in (1, 3, 2)]
    piece = picked[0] + arrived[0] + arrived[1] + arrived[2]
    row_pieces = [piece] + [shift(piece, "x", step) for step in (1, 2, 3)]

    light_rows, light_pair, head, tail = pl.pallas_call(
        local_kernel,
        out_shape=[array(rows, width), array(rows, 2 * width)] + [array(HALO, 2 * width)] * 2,
        in_specs=[vmem()] * 4,
        out_specs=[vmem()] * 4,
        cost_estimate=cost(6 * rows * width * model, 2 * rows * model + 6 * model * width),
        name="light_project",
    )(tokens, light_query, light_key, light_value)
    devices = blocks * x_size
    up = [(i, i + 1) for i in range(devices - 1)]
    before = lax.ppermute(tail, ALL_AXES, up)
    after = lax.ppermute(head, ALL_AXES, [(b, a) for a, b in up])
    light_mixed = pl.pallas_call(
        functools.partial(light_kernel, total=rows * devices),
        out_shape=array(rows, width),
        in_specs=[smem()] + [vmem()] * 4,
        out_specs=vmem(),
        scratch_shapes=[pltpu.VMEM((rows + 2 * HALO, 2 * width), bf16)],
        cost_estimate=cost(4 * rows * 512 * 256 * 4, 4 * rows * width * 2, 4 * rows * 512),
        name="light",
    )(first.reshape(1), light_rows, before, light_pair, after)

    bounds = jnp.arange(blocks + 1, dtype=jnp.int32) * block_len
    key_starts = jnp.sum((key_index[None, :] < bounds[:, None]).astype(jnp.int32), axis=1)
    query_starts = jnp.sum((query_index[None, :] < bounds[:, None]).astype(jnp.int32), axis=1)

    pairs = pl.pallas_call(
        pair_kernel,
        out_shape=array(y_size * key_cap, 2 * HDIM),
        in_specs=[smem()] + [vmem()] * 6,
        out_specs=vmem(),
        scratch_shapes=[pltpu.VMEM((key_cap, model), bf16)],
        cost_estimate=cost(4 * key_cap * model * heavy_width, 4 * model * heavy_width),
        name="key_value_heads",
    )(place, *row_pieces, heavy_key, heavy_value)
    column = exchange(pairs)

    *projected, query_slots = pl.pallas_call(
        project_kernel,
        out_shape=[array(query_cap, heavy_width)] * x_size
        + [jax.ShapeDtypeStruct((1, query_cap), jnp.int32)],
        in_specs=[smem()] + [vmem()] * 7,
        out_specs=[vmem()] * (x_size + 1),
        scratch_shapes=[
            pltpu.VMEM((model, heavy_width), bf16),
            pltpu.VMEM((x_size, rows, heavy_width), bf16),
        ],
        cost_estimate=cost(8 * query_cap * model * heavy_width, 8 * model * heavy_width),
        name="query_project",
    )(place, query_lines, tokens, heavy_query, *wq)
    q_in = [shift(projected[i + 1], "x", step) for i, step in enumerate((-1, 1, 2))]
    q_heads = pl.pallas_call(
        query_kernel,
        out_shape=array(y_size * query_cap // 2, 2 * HDIM),
        in_specs=[vmem()] * 4,
        out_specs=vmem(),
        cost_estimate=cost(4 * query_cap * heavy_width, 10 * query_cap * heavy_width),
        name="query_heads",
    )(projected[0], *q_in)
    q_column = exchange(q_heads)

    wo = gather_weights(heavy_out)

    ring = {0: column}
    for step in range(1, z_size // 2 + 1):
        if step == 3:
            ring[-2], key_starts, query_starts = lax.optimization_barrier(
                (ring[-2], key_starts, query_starts)
            )
        ring[-step] = shift(ring[-step + 1], "z", 1)
        if step < z_size // 2:
            ring[step] = shift(ring[step - 1], "z", -1)
    near_pairs = [ring[s] for s in Z_STEPS]
    far_pairs = [shift(ring[s], "c", 1) for s in Z_STEPS]

    key_total = 2 * z_size * column.shape[0]
    slots_total = y_size * query_cap + QTILE
    heads_out = pl.pallas_call(
        functools.partial(attention_kernel, sizes=(y_size, z_size)),
        out_shape=array(y_size * query_cap // 2, 2 * HDIM),
        in_specs=[smem()] * 3 + [vmem()] * (1 + 2 * z_size),
        out_specs=vmem(),
        scratch_shapes=[
            pltpu.VMEM((slots_total, 2 * HDIM), bf16),
            pltpu.VMEM((key_total + KCHUNK, 2 * HDIM), bf16),
            pltpu.VMEM((key_total + KCHUNK, 2 * HDIM), bf16),
            pltpu.VMEM((slots_total, 2 * HDIM), bf16),
        ],
        cost_estimate=cost(4 * 1024 * key_total * 256, 4 * key_total * HDIM, 1024 * key_total),
        name="heavy_attention",
    )(place, query_starts, key_starts, q_column, *near_pairs, *far_pairs)

    back = exchange(heads_out)
    groups = [back] + [shift(back, "x", step) for step in (1, -1, 2)]
    tile = 512

    def whole(*shape):
        return pl.BlockSpec(shape, lambda j: (0,) * len(shape))

    def columns(count):
        return pl.BlockSpec((count, tile), lambda j: (0, j))

    so_far = pl.pallas_call(
        own_kernel,
        grid=(model // tile,),
        out_shape=jax.ShapeDtypeStruct((rows, model), jnp.float32),
        in_specs=[
            whole(1, query_cap),
            whole(rows, width),
            columns(width),
            whole(y_size * query_cap // 2, 2 * HDIM),
            columns(heavy_width),
        ],
        out_specs=columns(rows),
        scratch_shapes=[pltpu.VMEM((rows, heavy_width), bf16)],
        cost_estimate=cost(2 * rows * 512 * model, 6 * rows * model),
        name="combine_own",
    )(query_slots, light_mixed, light_out, back, heavy_out)
    return pl.pallas_call(
        final_kernel,
        grid=(model // tile,),
        out_shape=array(rows, model),
        in_specs=[smem(), whole(1, query_cap), columns(rows)]
        + [whole(y_size * query_cap // 2, 2 * HDIM)] * 3
        + [columns(p.shape[0]) for p in wo],
        out_specs=columns(rows),
        scratch_shapes=[pltpu.VMEM((3, rows, heavy_width), bf16)],
        cost_estimate=cost(2 * rows * 768 * model, 10 * rows * model),
        name="combine",
    )(place, query_slots, so_far, *groups[1:], *wo)


def solution(mesh):
    torus = Mesh(mesh.devices.reshape(4, 8, 2, mesh.shape["head"]), ALL_AXES)
    return jax.shard_map(
        layer,
        mesh=torus,
        in_specs=(P(ALL_AXES, None),)
        + (P(),) * 6
        + (P(None, "x"),) * 3
        + (P("x", None),),
        out_specs=P(ALL_AXES, None),
        check_vma=False,
    )
```
